256 devices in a mesh: seq: 32 (over y, z), batch: 8 (over x, core).
Axes of the slice: x: 4, y: 4, z: 8, core: 2. Of those that a mesh axis runs over, the one named last changes fastest.
Arguments:
- queries: bfloat16 [32768, 4096], P(('batch', 'seq')), parts along dimension 0
- keys: bfloat16 [32768, 4096], P(('batch', 'seq')), parts along dimension 0
- values: bfloat16 [32768, 4096], P(('batch', 'seq')), parts along dimension 0, may hold values from -6 to 6
- out_grad: bfloat16 [32768, 4096], P(('batch', 'seq')), parts along dimension 0, may hold values from -6 to 6
- key_blocks: int32 [256, 64, 12], P('batch'), parts along dimension 0, may hold values from -1 to 63, as said below
- dilation: int32 [256], P('batch'), parts along dimension 0, may hold values from 1 to 729, as said below
Outputs:
- attended: bfloat16 [32768, 4096], P(('batch', 'seq')), parts along dimension 0
- queries_grad: bfloat16 [32768, 4096], P(('batch', 'seq')), parts along dimension 0
- keys_grad: bfloat16 [32768, 4096], P(('batch', 'seq')), parts along dimension 0
- values_grad: bfloat16 [32768, 4096], P(('batch', 'seq')), parts along dimension 0
The draws below stay inside these ranges and needn't reach their ends.
There are 8 independent parts, one for each index of `batch`. The reference program is written for one: setup_inputs(seed, part) draws one part's arguments, and reference() takes and returns one part's arrays. A program takes and returns all parts, laid end to end along the dimension named above; each array names one. Nothing has to cross between parts.
Inputs may be any that keep to these rules, and one draw needn't show every extreme that they name: `key_blocks`: in every row the first entry is the query block itself; the listed blocks are distinct, not after the query block, and stand before the -1 entries. Some head lists 12 blocks for each of its last query blocks. `dilation`: every value is a power of three.
All inputs are finite; a program needn't handle non-finite values.
Results may differ from the reference program's by a relative error of at most 0.012.
Values may be sent and summed in bfloat16 or wider, within the bound.
No kernel may reach another device: no remote copies, remote signals or barrier semaphores. Data moves between devices by JAX's collectives and lax.ppermute only.
A program may use at most 64 MiB of HBM per device.

```python
import math
import jax
import jax.numpy as jnp
from jax import lax

HEADS = 32
HEAD_DIM = 128
BLOCK = 64
SLOTS = 12
D = 4096
SEQLEN = 4096
QBLOCKS = 64


def drawn_pair(key):
    base = jax.random.fold_in(key, 7)
    first, second = jax.random.split(base, 2)
    query_noise = jnp.clip(jax.random.normal(first, (SEQLEN, HEADS * HEAD_DIM), jnp.float32), -6.0, 6.0)
    key_noise = jnp.clip(jax.random.normal(second, (SEQLEN, HEADS * HEAD_DIM), jnp.float32), -6.0, 6.0)
    return (query_noise, key_noise)


def draw_queries(key, part):
    return drawn_pair(key)[0].astype(jnp.bfloat16)


def draw_keys(key, part):
    return drawn_pair(key)[1].astype(jnp.bfloat16)


def sparse_pattern(key):
    base = jax.random.fold_in(key, 19)
    key_one, key_two, key_three, key_four = jax.random.split(base, 4)
    head_ids = jnp.arange(HEADS, dtype=jnp.int32)
    heavy = jax.random.randint(key_four, (), 0, HEADS, dtype=jnp.int32)
    powers = jnp.array([1, 3, 9, 27, 81, 243, 729], jnp.int32)
    spacing = powers[jax.random.randint(key_one, (HEADS,), 0, 7, dtype=jnp.int32)]
    spacing = jnp.where(head_ids == heavy, 1, jnp.where(head_ids == (heavy + 1) % HEADS, 729, spacing))
    stride = jax.random.randint(key_two, (HEADS,), 1, 3, dtype=jnp.int32)
    stride = jnp.where(head_ids == heavy, 1, stride)
    reaches = jnp.array([2, 3, 4, 6, 8], jnp.int32)
    reach = reaches[jax.random.randint(key_three, (HEADS,), 0, 5, dtype=jnp.int32)]
    reach = jnp.where(head_ids == heavy, SLOTS, reach)
    query_ids = jnp.arange(QBLOCKS, dtype=jnp.int32)[None, :, None]
    slot_ids = jnp.arange(SLOTS, dtype=jnp.int32)[None, None, :]
    listed = query_ids - slot_ids * stride[:, None, None]
    valid = (slot_ids < reach[:, None, None]) & (listed >= 0)
    return (spacing, jnp.where(valid, listed, -1).astype(jnp.int32))


def draw_key_blocks(key, part):
    return sparse_pattern(key)[1]


def draw_dilation(key, part):
    return sparse_pattern(key)[0]


def shard_levels(rng, extent, pieces, low, largest):
    loudness, own = 1.0, jax.random.fold_in(rng, 6)
    for dim, blocks in pieces:
        heights = jnp.exp(jax.random.uniform(jax.random.fold_in(own, dim), (blocks,), jnp.float32, low / len(pieces), largest / len(pieces)))
        loudness = loudness * jnp.repeat(heights, extent[dim] // blocks).reshape([-1 if axis == dim else 1 for axis in range(len(extent))])
    return loudness


def centred(rng, dims, deviation, most, pieces=(), held_as=jnp.bfloat16):
    level = shard_levels(rng, dims, pieces, -0.22, 0.18) if pieces else 1.0
    values = jax.random.normal(rng, dims, jnp.float32) * deviation * level
    return jnp.minimum(jnp.maximum(values, -most), most).astype(held_as)


def setup_inputs(seed: int = 0, part: int = 0) -> dict:
    key_list = jax.random.split(jax.random.key(seed), 7)
    part_splits = jax.random.split(jax.random.fold_in(key_list[6], part), 7)
    return {
        "queries": draw_queries(jax.random.fold_in(jax.random.fold_in(key_list[6], part), 71), part),
        "keys": draw_keys(jax.random.fold_in(jax.random.fold_in(key_list[6], part), 71), part),
        "values": centred(part_splits[2], (SEQLEN, D), 1.0, 6.0, ((0, 32),)),
        "out_grad": centred(part_splits[3], (SEQLEN, D), 1.0, 6.0, ((0, 32),)),
        "key_blocks": draw_key_blocks(jax.random.fold_in(jax.random.fold_in(key_list[6], part), 71), part),
        "dilation": draw_dilation(jax.random.fold_in(jax.random.fold_in(key_list[6], part), 71), part),
    }


very_low = -1e+30

def split_heads(rows):
    return rows.reshape(QBLOCKS, BLOCK, HEADS, HEAD_DIM).transpose(2, 0, 1, 3)

def join_heads(per_head):
    return per_head.transpose(1, 2, 0, 3).reshape(SEQLEN, HEADS * HEAD_DIM)

def one_head(operands):
    head_queries, head_keys, head_values, head_grads, block_rows, spacing = operands
    score_scale = 1.0 / math.sqrt(HEAD_DIM)
    valid = block_rows >= 0
    chosen = jnp.maximum(block_rows, 0).astype(jnp.int32)
    keys_tiles = head_keys[chosen].reshape(QBLOCKS, SLOTS * BLOCK, HEAD_DIM).astype(jnp.float32)
    values_tiles = head_values[chosen].reshape(QBLOCKS, SLOTS * BLOCK, HEAD_DIM).astype(jnp.float32)
    query_ids = jnp.arange(QBLOCKS, dtype=jnp.int32)
    offsets = lax.broadcasted_iota(jnp.int32, (BLOCK, BLOCK), 0) - lax.broadcasted_iota(jnp.int32, (BLOCK, BLOCK), 1)
    distance = ((query_ids[:, None] - chosen) * BLOCK)[:, None, :, None] + offsets[None, :, None, :]
    allowed = valid[:, None, :, None] & (distance >= 0) & (distance % spacing == 0)
    allowed = allowed.reshape(QBLOCKS, BLOCK, SLOTS * BLOCK)
    queries32 = head_queries.astype(jnp.float32)
    grads32 = head_grads.astype(jnp.float32)
    scores = jnp.einsum('gae,gke->gak', queries32, keys_tiles) * score_scale
    scores = jnp.where(allowed, scores, very_low)
    row_top = lax.optimization_barrier(jnp.max(scores, axis=2, keepdims=True))
    expos = jnp.exp(scores - row_top)
    weights = expos / lax.optimization_barrier(jnp.sum(expos, axis=2, keepdims=True))
    weights16 = lax.optimization_barrier(weights.astype(jnp.bfloat16))
    weights_back = weights16.astype(jnp.float32)
    attended = jnp.einsum('gak,gke->gae', weights_back, values_tiles).astype(jnp.bfloat16)
    attended_back = lax.optimization_barrier(attended).astype(jnp.float32)
    delta = lax.optimization_barrier(jnp.sum(grads32 * attended_back, axis=2, keepdims=True))
    dweights = jnp.einsum('gae,gke->gak', grads32, values_tiles)
    dscores16 = lax.optimization_barrier((weights * (dweights - delta)).astype(jnp.bfloat16))
    dscores_back = dscores16.astype(jnp.float32)
    queries_grad = (jnp.einsum('gak,gke->gae', dscores_back, keys_tiles) * score_scale).astype(jnp.bfloat16)
    keys_parts = (jnp.einsum('gak,gae->gke', dscores_back, queries32) * score_scale).reshape(QBLOCKS * SLOTS, BLOCK, HEAD_DIM)
    values_parts = jnp.einsum('gak,gae->gke', weights_back, grads32).reshape(QBLOCKS * SLOTS, BLOCK, HEAD_DIM)
    flat_ids = chosen.reshape(-1)
    keys_grad = jnp.zeros((QBLOCKS, BLOCK, HEAD_DIM), jnp.float32).at[flat_ids].add(keys_parts).astype(jnp.bfloat16)
    values_grad = jnp.zeros((QBLOCKS, BLOCK, HEAD_DIM), jnp.float32).at[flat_ids].add(values_parts).astype(jnp.bfloat16)
    return (attended, queries_grad, keys_grad, values_grad)

def reference(queries, keys, values, out_grad, key_blocks, dilation):
    results = lax.map(one_head, (split_heads(queries), split_heads(keys), split_heads(values), split_heads(out_grad), key_blocks, dilation))
    return (join_heads(results[0]), join_heads(results[1]), join_heads(results[2]), join_heads(results[3]))
```

```python
import math

import jax
import jax.numpy as jnp
from jax import lax
from jax.experimental import pallas as pl
from jax.experimental.pallas import tpu as pltpu
from jax.sharding import PartitionSpec as P

HEADS = 32
HEAD_DIM = 128
BLOCK = 64
PAIR = 2 * BLOCK
SLOTS = 12
SCALE = 1.0 / math.sqrt(HEAD_DIM)
VERY_LOW = -1e30
PAIRS_PER_STEP = 2
VMEM_LIMIT = 40 << 20

f32 = jnp.float32
bf16 = jnp.bfloat16
NT = (((1,), (1,)), ((), ()))
NN = (((1,), (0,)), ((), ()))


def index_tables(lists, spacing):
    blocks = lists.shape[0]
    ids = jnp.arange(blocks, dtype=jnp.int32)[:, None]
    valid = lists >= 0
    load = jnp.maximum(lists, 0)
    store = jnp.where(valid, lists, blocks)
    residue = jnp.where(valid, jnp.mod((load - ids) * BLOCK, spacing), -1)
    residue = residue.reshape(blocks // 2, 2, SLOTS).transpose(0, 2, 1)
    residue = jnp.broadcast_to(residue[:, :, :, None], (blocks // 2, SLOTS, 2, BLOCK))
    residue = residue.reshape(blocks // 2, SLOTS, PAIR)
    residue = jnp.pad(residue, ((0, 0), (0, 16 - SLOTS), (0, 0)), constant_values=-1)
    key_at = lax.broadcasted_iota(jnp.int32, (BLOCK, PAIR), 0)
    query_at = lax.broadcasted_iota(jnp.int32, (BLOCK, PAIR), 1) % BLOCK
    offsets = jnp.mod(query_at - key_at, spacing)
    return load, store, residue, jnp.stack([jnp.where(query_at >= key_at, offsets, -2), offsets])


def side_by_side(rows):
    zero = jnp.zeros((BLOCK, HEAD_DIM), rows.dtype)
    return jnp.concatenate(
        [
            jnp.concatenate([rows[:BLOCK], zero], 1),
            jnp.concatenate([zero, rows[BLOCK:]], 1),
        ],
        0,
    )


def listed_pair(blocks_ref, load_ref, first):
    return jnp.concatenate(
        [
            jnp.concatenate(
                [blocks_ref[load_ref[first, s]], blocks_ref[load_ref[first + 1, s]]], 1
            )
            for s in range(SLOTS)
        ],
        0,
    )


def store_rows(out_ref, weights_t, blocks_ref, load_ref, pair, scale):
    weights = weights_t.T
    for half in range(2):
        rows = jnp.concatenate(
            [blocks_ref[load_ref[2 * pair + half, s]] for s in range(SLOTS)], 0
        )
        out = lax.dot_general(
            weights[half * BLOCK : (half + 1) * BLOCK], rows, NN, preferred_element_type=f32
        )
        if scale is not None:
            out = out * scale
        start = pl.multiple_of(pair * PAIR + half * BLOCK, BLOCK)
        out_ref[pl.ds(start, BLOCK), :] = out.astype(bf16)


def add_to_listed(sum_ref, parts, store_ref, first, group=4):
    for half in range(2):
        for start in range(0, SLOTS, group):
            slots = range(start, start + group)
            blocks = [store_ref[first + half, s] for s in slots]
            before = [sum_ref[b] for b in blocks]
            for s, b, old in zip(slots, blocks, before):
                sum_ref[b] = (
                    old
                    + parts[
                        s * BLOCK : (s + 1) * BLOCK, half * HEAD_DIM : (half + 1) * HEAD_DIM
                    ]
                )


def pair_forward(load_ref, residue_ref, offsets_ref, q_ref, k_ref, v_ref, weights_ref, o_ref, pair, slot):
    start = pl.multiple_of(pair * PAIR, PAIR)
    q_diag = side_by_side(q_ref[pl.ds(start, PAIR), :])
    keys = listed_pair(k_ref, load_ref, 2 * pair)
    scores = lax.dot_general(keys, q_diag, NT, preferred_element_type=f32)
    residue = residue_ref[pair]
    masked = [
        jnp.where(
            offsets_ref[0 if s == 0 else 1] == residue[s : s + 1],
            scores[s * BLOCK : (s + 1) * BLOCK],
            VERY_LOW,
        )
        for s in range(SLOTS)
    ]
    top = masked[0]
    for part in masked[1:]:
        top = jnp.maximum(top, part)
    top = jnp.max(top, axis=0, keepdims=True)
    expos = [jnp.exp2((part - top) * (SCALE * math.log2(math.e))) for part in masked]
    total = expos[0]
    for part in expos[1:]:
        total = total + part
    inverse = 1.0 / jnp.sum(total, axis=0, keepdims=True)
    weights_t = jnp.concatenate([(part * inverse).astype(bf16) for part in expos], 0)
    weights_ref[slot] = weights_t
    store_rows(o_ref, weights_t, v_ref, load_ref, pair, None)


def pair_backward(
    load_ref, store_ref, weights_ref, q_ref, k_ref, v_ref, g_ref, o_ref, dq_ref, k_sum, v_sum, pair, slot
):
    start = pl.multiple_of(pair * PAIR, PAIR)
    grads = g_ref[pl.ds(start, PAIR), :]
    outs = o_ref[pl.ds(start, PAIR), :]
    delta = jnp.sum((grads.astype(f32) * outs.astype(f32)).T, axis=0, keepdims=True)
    g_diag = side_by_side(grads)
    q_diag = side_by_side(q_ref[pl.ds(start, PAIR), :])
    values = listed_pair(v_ref, load_ref, 2 * pair)
    dweights = lax.dot_general(values, g_diag, NT, preferred_element_type=f32)
    weights_t = weights_ref[slot]
    dscores = (weights_t.astype(f32) * (dweights - delta)).astype(bf16)
    add_to_listed(
        v_sum,
        lax.dot_general(weights_t, g_diag, NN, preferred_element_type=f32),
        store_ref,
        2 * pair,
    )
    add_to_listed(
        k_sum,
        lax.dot_general(dscores, q_diag, NN, preferred_element_type=f32),
        store_ref,
        2 * pair,
    )
    store_rows(dq_ref, dscores, k_ref, load_ref, pair, SCALE)


SCALARS = pl.BlockSpec(memory_space=pltpu.SMEM)


def resident(shape):
    zeros = (0,) * len(shape)
    return pl.BlockSpec(shape, lambda step: zeros, pipeline_mode=pl.Buffered(1))


def head_forward(q, k, v, tables):
    load, _, residue, offsets = tables
    pairs = q.shape[0] // PAIR
    weights_shape = (pairs, SLOTS * BLOCK, PAIR)

    def body(load_ref, residue_ref, offsets_ref, q_ref, k_ref, v_ref, weights_ref, o_ref):
        for u in range(PAIRS_PER_STEP):
            pair = pl.program_id(0) * PAIRS_PER_STEP + u
            pair_forward(
                load_ref, residue_ref, offsets_ref, q_ref, k_ref, v_ref, weights_ref, o_ref, pair, u
            )

    return pl.pallas_call(
        body,
        grid=(pairs // PAIRS_PER_STEP,),
        in_specs=[SCALARS]
        + [resident(x.shape) for x in (residue, offsets, q, k, v)],
        out_specs=[
            pl.BlockSpec((PAIRS_PER_STEP,) + weights_shape[1:], lambda step: (step, 0, 0)),
            resident(q.shape),
        ],
        out_shape=[
            jax.ShapeDtypeStruct(weights_shape, bf16),
            jax.ShapeDtypeStruct(q.shape, bf16),
        ],
        cost_estimate=pl.CostEstimate(
            flops=20_000_000_000, transcendentals=3_000_000, bytes_accessed=10_000_000
        ),
        compiler_params=pltpu.CompilerParams(vmem_limit_bytes=VMEM_LIMIT),
        name="head_forward",
    )(load, residue, offsets, q, k, v)


def head_backward(q, k, v, g, o, weights, tables):
    load, store, _, _ = tables
    pairs = q.shape[0] // PAIR
    blocks = q.shape[0] // BLOCK

    def body(
        load_ref, store_ref, weights_ref, q_ref, k_ref, v_ref, g_ref, o_ref,
        dq_ref, dk_ref, dv_ref, k_sum, v_sum,
    ):
        @pl.when(pl.program_id(0) == 0)
        def _():
            k_sum[...] = jnp.zeros(k_sum.shape, f32)
            v_sum[...] = jnp.zeros(v_sum.shape, f32)

        for u in range(PAIRS_PER_STEP):
            pair = pl.program_id(0) * PAIRS_PER_STEP + u
            pair_backward(
                load_ref, store_ref, weights_ref, q_ref, k_ref, v_ref, g_ref, o_ref,
                dq_ref, k_sum, v_sum, pair, u,
            )

        @pl.when(pl.program_id(0) == pl.num_programs(0) - 1)
        def _():
            dk_ref[...] = (k_sum[:blocks] * SCALE).astype(bf16)
            dv_ref[...] = v_sum[:blocks].astype(bf16)

    return pl.pallas_call(
        body,
        grid=(pairs // PAIRS_PER_STEP,),
        in_specs=[
            SCALARS,
            SCALARS,
            pl.BlockSpec((PAIRS_PER_STEP, SLOTS * BLOCK, PAIR), lambda step: (step, 0, 0)),
        ]
        + [resident(x.shape) for x in (q, k, v, g, o)],
        out_specs=[resident(q.shape), resident(k.shape), resident(v.shape)],
        out_shape=[jax.ShapeDtypeStruct(x.shape, bf16) for x in (q, k, v)],
        scratch_shapes=[pltpu.VMEM((blocks + 1, BLOCK, HEAD_DIM), f32)] * 2,
        cost_estimate=pl.CostEstimate(
            flops=24_000_000_000, transcendentals=0, bytes_accessed=16_000_000
        ),
        compiler_params=pltpu.CompilerParams(vmem_limit_bytes=VMEM_LIMIT),
        name="head_backward",
    )(load, store, weights, q, k, v, g, o)


def to_heads(rows):
    return lax.all_to_all(rows, "seq", split_axis=1, concat_axis=0, tiled=True)


def to_tokens(head):
    devices = lax.axis_size("seq")
    by_device = head.reshape(devices, -1, HEAD_DIM)
    received = lax.all_to_all(by_device, "seq", split_axis=0, concat_axis=0, tiled=True)
    return received.transpose(1, 0, 2).reshape(by_device.shape[1], devices * HEAD_DIM)


def blocked(head):
    return head.reshape(-1, BLOCK, HEAD_DIM)


def local(queries, keys, values, out_grad, key_blocks, dilation):
    my_head = lax.axis_index("seq")
    tables = index_tables(
        lax.dynamic_index_in_dim(key_blocks, my_head, 0, keepdims=False),
        lax.dynamic_index_in_dim(dilation, my_head, 0, keepdims=False),
    )
    q = to_heads(queries)
    k = blocked(to_heads(keys))
    v = blocked(to_heads(values))
    g = to_heads(out_grad)
    weights, o = head_forward(q, k, v, tables)
    dq, dk, dv = head_backward(q, k, v, g, o, weights, tables)
    return to_tokens(o), to_tokens(dq), to_tokens(dk), to_tokens(dv)


def solution(mesh):
    rows = P(("batch", "seq"), None)
    return jax.shard_map(
        local,
        mesh=mesh,
        in_specs=(rows, rows, rows, rows, P("batch", None, None), P("batch")),
        out_specs=(rows, rows, rows, rows),
        check_vma=False,
    )
```

```python
import math

import jax
import jax.numpy as jnp
from jax import lax
from jax.experimental import pallas as pl
from jax.experimental.pallas import tpu as pltpu
from jax.sharding import PartitionSpec as P

HEADS = 32
HEAD_DIM = 128
BLOCK = 64
PAIR = 2 * BLOCK
SLOTS = 12
SCALE = 1.0 / math.sqrt(HEAD_DIM)
VERY_LOW = -1e30
PAIRS_PER_STEP = 2
HEADS_PER_STEP = 16
VMEM_LIMIT = 40 << 20

f32 = jnp.float32
bf16 = jnp.bfloat16
NT = (((1,), (1,)), ((), ()))
NN = (((1,), (0,)), ((), ()))


def index_tables(lists, spacing):
    blocks = lists.shape[0]
    ids = jnp.arange(blocks, dtype=jnp.int32)[:, None]
    valid = lists >= 0
    listed_block = jnp.maximum(lists, 0)
    load = listed_block // 2 * 6 + listed_block % 2
    store = jnp.where(valid, lists, blocks)
    residue = jnp.where(valid, jnp.mod((listed_block - ids) * BLOCK, spacing), -1)
    residue = residue.reshape(blocks // 2, 2, SLOTS).transpose(0, 2, 1)
    residue = jnp.broadcast_to(residue[:, :, :, None], (blocks // 2, SLOTS, 2, BLOCK))
    residue = residue.reshape(blocks // 2, SLOTS, PAIR)
    residue = jnp.pad(residue, ((0, 0), (0, 16 - SLOTS), (0, 0)), constant_values=-1)
    key_at = lax.broadcasted_iota(jnp.int32, (BLOCK, PAIR), 0)
    query_at = lax.broadcasted_iota(jnp.int32, (BLOCK, PAIR), 1) % BLOCK
    offsets = jnp.mod(query_at - key_at, spacing)
    return load, store, residue, jnp.stack([jnp.where(query_at >= key_at, offsets, -2), offsets])


def side_by_side(rows):
    zero = jnp.zeros((BLOCK, HEAD_DIM), rows.dtype)
    return jnp.concatenate(
        [
            jnp.concatenate([rows[:BLOCK], zero], 1),
            jnp.concatenate([zero, rows[BLOCK:]], 1),
        ],
        0,
    )


def listed(packed_ref, load_ref, block, array):
    return [packed_ref[load_ref[block, s] + 2 * array] for s in range(SLOTS)]


def listed_pair(packed_ref, load_ref, first, array):
    left = listed(packed_ref, load_ref, first, array)
    right = listed(packed_ref, load_ref, first + 1, array)
    return jnp.concatenate(
        [jnp.concatenate([a, b], 1) for a, b in zip(left, right)], 0
    )


def pair_queries(packed_ref, pair):
    return packed_ref[pl.ds(6 * pair, 2)].reshape(PAIR, HEAD_DIM)


def rows_of_pair(weights_t, packed_ref, load_ref, pair, array):
    weights = weights_t.T
    outs = []
    for half in range(2):
        rows = jnp.concatenate(listed(packed_ref, load_ref, 2 * pair + half, array), 0)
        outs.append(
            lax.dot_general(
                weights[half * BLOCK : (half + 1) * BLOCK], rows, NN, preferred_element_type=f32
            )
        )
    return jnp.concatenate(outs, 0)


def add_to_listed(sum_ref, parts, store_ref, first, group=4):
    for half in range(2):
        for start in range(0, SLOTS, group):
            slots = range(start, start + group)
            blocks = [store_ref[first + half, s] for s in slots]
            before = [sum_ref[b] for b in blocks]
            for s, b, old in zip(slots, blocks, before):
                sum_ref[b] = (
                    old
                    + parts[
                        s * BLOCK : (s + 1) * BLOCK, half * HEAD_DIM : (half + 1) * HEAD_DIM
                    ]
                )


def pair_forward(load_ref, residue_ref, offsets_ref, qkv_ref, weights_ref, o_ref, pair, slot):
    q_diag = side_by_side(pair_queries(qkv_ref, pair))
    keys = listed_pair(qkv_ref, load_ref, 2 * pair, 1)
    scores = lax.dot_general(keys, q_diag, NT, preferred_element_type=f32)
    residue = residue_ref[pair]
    masked = [
        jnp.where(
            offsets_ref[0 if s == 0 else 1] == residue[s : s + 1],
            scores[s * BLOCK : (s + 1) * BLOCK],
            VERY_LOW,
        )
        for s in range(SLOTS)
    ]
    top = masked[0]
    for part in masked[1:]:
        top = jnp.maximum(top, part)
    top = jnp.max(top, axis=0, keepdims=True)
    expos = [jnp.exp2((part - top) * (SCALE * math.log2(math.e))) for part in masked]
    total = expos[0]
    for part in expos[1:]:
        total = total + part
    inverse = 1.0 / jnp.sum(total, axis=0, keepdims=True)
    weights_t = jnp.concatenate([(part * inverse).astype(bf16) for part in expos], 0)
    weights_ref[slot] = weights_t
    o_ref[pair] = rows_of_pair(weights_t, qkv_ref, load_ref, pair, 2).astype(bf16)


def pair_backward(
    load_ref, store_ref, weights_ref, qkv_ref, g_ref, o_ref, grads_ref, k_sum, v_sum, pair, slot
):
    grads = g_ref[pair]
    delta = jnp.sum((grads.astype(f32) * o_ref[pair].astype(f32)).T, axis=0, keepdims=True)
    g_diag = side_by_side(grads)
    q_diag = side_by_side(pair_queries(qkv_ref, pair))
    values = listed_pair(qkv_ref, load_ref, 2 * pair, 2)
    dweights = lax.dot_general(values, g_diag, NT, preferred_element_type=f32)
    weights_t = weights_ref[slot]
    dscores = (weights_t.astype(f32) * (dweights - delta)).astype(bf16)
    add_to_listed(
        v_sum,
        lax.dot_general(weights_t, g_diag, NN, preferred_element_type=f32),
        store_ref,
        2 * pair,
    )
    add_to_listed(
        k_sum,
        lax.dot_general(dscores, q_diag, NN, preferred_element_type=f32),
        store_ref,
        2 * pair,
    )
    grads_ref[pair, 0] = (rows_of_pair(dscores, qkv_ref, load_ref, pair, 1) * SCALE).astype(bf16)


SCALARS = pl.BlockSpec(memory_space=pltpu.SMEM)


def resident(shape):
    zeros = (0,) * len(shape)
    return pl.BlockSpec(shape, lambda step: zeros, pipeline_mode=pl.Buffered(1))


def head_forward(qkv, tables):
    load, _, residue, offsets = tables
    pairs = residue.shape[0]
    weights_shape = (pairs, SLOTS * BLOCK, PAIR)
    out_shape = (pairs, PAIR, HEAD_DIM)

    def body(load_ref, residue_ref, offsets_ref, qkv_ref, weights_ref, o_ref):
        for u in range(PAIRS_PER_STEP):
            pair = pl.program_id(0) * PAIRS_PER_STEP + u
            pair_forward(
                load_ref, residue_ref, offsets_ref, qkv_ref, weights_ref, o_ref, pair, u
            )

    return pl.pallas_call(
        body,
        grid=(pairs // PAIRS_PER_STEP,),
        in_specs=[SCALARS] + [resident(x.shape) for x in (residue, offsets, qkv)],
        out_specs=[
            pl.BlockSpec((PAIRS_PER_STEP,) + weights_shape[1:], lambda step: (step, 0, 0)),
            resident(out_shape),
        ],
        out_shape=[
            pltpu.HBM(weights_shape, bf16),
            jax.ShapeDtypeStruct(out_shape, bf16),
        ],
        cost_estimate=pl.CostEstimate(
            flops=20_000_000_000, transcendentals=3_000_000, bytes_accessed=10_000_000
        ),
        compiler_params=pltpu.CompilerParams(vmem_limit_bytes=VMEM_LIMIT),
        name="head_forward",
    )(load, residue, offsets, qkv)


def head_backward(qkv, g, o, weights, tables):
    load, store, _, _ = tables
    pairs = g.shape[0]
    blocks = 2 * pairs
    grads_shape = (pairs, 3, PAIR, HEAD_DIM)

    def body(
        load_ref, store_ref, weights_ref, qkv_ref, g_ref, o_ref, grads_ref, k_sum, v_sum
    ):
        @pl.when(pl.program_id(0) == 0)
        def _():
            k_sum[...] = jnp.zeros(k_sum.shape, f32)
            v_sum[...] = jnp.zeros(v_sum.shape, f32)

        for u in range(PAIRS_PER_STEP):
            pair = pl.program_id(0) * PAIRS_PER_STEP + u
            pair_backward(
                load_ref, store_ref, weights_ref, qkv_ref, g_ref, o_ref, grads_ref,
                k_sum, v_sum, pair, u,
            )

        @pl.when(pl.program_id(0) == pl.num_programs(0) - 1)
        def _():
            by_pair = (pairs, PAIR, HEAD_DIM)
            grads_ref[:, 1] = (k_sum[:blocks] * SCALE).astype(bf16).reshape(by_pair)
            grads_ref[:, 2] = v_sum[:blocks].astype(bf16).reshape(by_pair)

    return pl.pallas_call(
        body,
        grid=(pairs // PAIRS_PER_STEP,),
        in_specs=[
            SCALARS,
            SCALARS,
            pl.BlockSpec((PAIRS_PER_STEP, SLOTS * BLOCK, PAIR), lambda step: (step, 0, 0)),
        ]
        + [resident(x.shape) for x in (qkv, g, o)],
        out_specs=resident(grads_shape),
        out_shape=jax.ShapeDtypeStruct(grads_shape, bf16),
        scratch_shapes=[pltpu.VMEM((blocks + 1, BLOCK, HEAD_DIM), f32)] * 2,
        cost_estimate=pl.CostEstimate(
            flops=24_000_000_000, transcendentals=0, bytes_accessed=16_000_000
        ),
        compiler_params=pltpu.CompilerParams(vmem_limit_bytes=VMEM_LIMIT),
        name="head_backward",
    )(load, store, weights, qkv, g, o)


def exchange(by_device):
    return lax.all_to_all(by_device, "seq", split_axis=0, concat_axis=0, tiled=True)


def in_hbm(array):
    return pltpu.with_memory_space_constraint(array, pltpu.HBM)


def pack_heads(*arrays):
    tokens, width = arrays[0].shape
    number = len(arrays)

    def body(*refs):
        for a in range(number):
            for h in range(HEADS_PER_STEP):
                refs[number][h, a] = refs[a][:, h * HEAD_DIM : (h + 1) * HEAD_DIM]

    return pl.pallas_call(
        body,
        grid=(width // HEAD_DIM // HEADS_PER_STEP,),
        in_specs=[pl.BlockSpec((tokens, HEADS_PER_STEP * HEAD_DIM), lambda step: (0, step))]
        * number,
        out_specs=pl.BlockSpec(
            (HEADS_PER_STEP, number, tokens, HEAD_DIM), lambda step: (step, 0, 0, 0)
        ),
        out_shape=pltpu.HBM((width // HEAD_DIM, number, tokens, HEAD_DIM), bf16),
        compiler_params=pltpu.CompilerParams(vmem_limit_bytes=24 << 20),
        name="pack_heads",
    )(*[in_hbm(x) for x in arrays])


def unpack_heads(packed):
    heads, number, tokens, _ = packed.shape

    def body(packed_ref, *out_refs):
        for a in range(number):
            for h in range(HEADS_PER_STEP):
                out_refs[a][:, h * HEAD_DIM : (h + 1) * HEAD_DIM] = packed_ref[h, a]

    return pl.pallas_call(
        body,
        grid=(heads // HEADS_PER_STEP,),
        in_specs=[
            pl.BlockSpec((HEADS_PER_STEP, number, tokens, HEAD_DIM), lambda step: (step, 0, 0, 0))
        ],
        out_specs=[pl.BlockSpec((tokens, HEADS_PER_STEP * HEAD_DIM), lambda step: (0, step))]
        * number,
        out_shape=[jax.ShapeDtypeStruct((tokens, heads * HEAD_DIM), bf16)] * number,
        compiler_params=pltpu.CompilerParams(vmem_limit_bytes=24 << 20),
        name="unpack_heads",
    )(packed)


def local(queries, keys, values, out_grad, key_blocks, dilation):
    my_head = lax.axis_index("seq")
    tables = index_tables(
        lax.dynamic_index_in_dim(key_blocks, my_head, 0, keepdims=False),
        lax.dynamic_index_in_dim(dilation, my_head, 0, keepdims=False),
    )
    qkv = exchange(pack_heads(queries, keys, values)).reshape(-1, BLOCK, HEAD_DIM)
    g = exchange(pack_heads(out_grad)).reshape(-1, PAIR, HEAD_DIM)
    weights, o = head_forward(qkv, tables)
    attended = exchange(o[:, None])
    grads = exchange(head_backward(qkv, g, o, weights, tables))
    return tuple(unpack_heads(attended)) + tuple(unpack_heads(grads))


def solution(mesh):
    rows = P(("batch", "seq"), None)
    return jax.shard_map(
        local,
        mesh=mesh,
        in_specs=(rows, rows, rows, rows, P("batch", None, None), P("batch")),
        out_specs=(rows, rows, rows, rows),
        check_vma=False,
    )
```

```python
import math

import jax
import jax.numpy as jnp
from jax import lax
from jax.experimental import pallas as pl
from jax.experimental.pallas import tpu as pltpu
from jax.sharding import PartitionSpec as P

HEADS = 32
HEAD_DIM = 128
BLOCK = 64
PAIR = 2 * BLOCK
SLOTS = 12
SCALE = 1.0 / math.sqrt(HEAD_DIM)
VERY_LOW = -1e30
PAIRS_PER_STEP = 8
HEADS_PER_STEP = 16
VMEM_LIMIT = 30 << 20

f32 = jnp.float32
bf16 = jnp.bfloat16
NT = (((1,), (1,)), ((), ()))
NN = (((1,), (0,)), ((), ()))


def index_tables(lists, spacing):
    blocks = lists.shape[0]
    ids = jnp.arange(blocks, dtype=jnp.int32)[:, None]
    valid = lists >= 0
    listed_block = jnp.maximum(lists, 0)
    load = listed_block // 2 * 6 + listed_block % 2
    store = jnp.where(valid, lists, blocks)
    residue = jnp.where(valid, jnp.mod((listed_block - ids) * BLOCK, spacing), -1)
    residue = residue.reshape(blocks // 2, 2, SLOTS).transpose(0, 2, 1)
    residue = jnp.broadcast_to(residue[:, :, :, None], (blocks // 2, SLOTS, 2, BLOCK))
    residue = residue.reshape(blocks // 2, SLOTS, PAIR)
    residue = jnp.pad(residue, ((0, 0), (0, 16 - SLOTS), (0, 0)), constant_values=-1)
    key_at = lax.broadcasted_iota(jnp.int32, (BLOCK, PAIR), 0)
    query_at = lax.broadcasted_iota(jnp.int32, (BLOCK, PAIR), 1) % BLOCK
    offsets = jnp.mod(query_at - key_at, spacing)
    return load, store, residue, jnp.stack([jnp.where(query_at >= key_at, offsets, -2), offsets])


def side_by_side(rows):
    zero = jnp.zeros((BLOCK, HEAD_DIM), rows.dtype)
    return jnp.concatenate(
        [
            jnp.concatenate([rows[:BLOCK], zero], 1),
            jnp.concatenate([zero, rows[BLOCK:]], 1),
        ],
        0,
    )


def listed(packed_ref, load_ref, block, array):
    return [packed_ref[load_ref[block, s] + 2 * array] for s in range(SLOTS)]


def listed_pair(packed_ref, load_ref, first, array):
    left = listed(packed_ref, load_ref, first, array)
    right = listed(packed_ref, load_ref, first + 1, array)
    return jnp.concatenate(
        [jnp.concatenate([a, b], 1) for a, b in zip(left, right)], 0
    )


def pair_queries(packed_ref, pair):
    return packed_ref[pl.ds(6 * pair, 2)].reshape(PAIR, HEAD_DIM)


def rows_of_pair(weights_t, packed_ref, load_ref, pair, array):
    weights = weights_t.T
    outs = []
    for half in range(2):
        rows = jnp.concatenate(listed(packed_ref, load_ref, 2 * pair + half, array), 0)
        outs.append(
            lax.dot_general(
                weights[half * BLOCK : (half + 1) * BLOCK], rows, NN, preferred_element_type=f32
            )
        )
    return jnp.concatenate(outs, 0)


def add_to_listed(sum_ref, parts, store_ref, first, group=4):
    for half in range(2):
        for start in range(0, SLOTS, group):
            slots = range(start, start + group)
            blocks = [store_ref[first + half, s] for s in slots]
            before = [sum_ref[b] for b in blocks]
            for s, b, old in zip(slots, blocks, before):
                sum_ref[b] = (
                    old
                    + parts[
                        s * BLOCK : (s + 1) * BLOCK, half * HEAD_DIM : (half + 1) * HEAD_DIM
                    ]
                )


def pair_scores(load_ref, qkv_ref, pair):
    q_diag = side_by_side(pair_queries(qkv_ref, pair))
    keys = listed_pair(qkv_ref, load_ref, 2 * pair, 1)
    return lax.dot_general(keys, q_diag, NT, preferred_element_type=f32)


def pair_weights(residue_ref, offsets_ref, scores, pair):
    residue = residue_ref[pair]
    masked = [
        jnp.where(
            offsets_ref[0 if s == 0 else 1] == residue[s : s + 1],
            scores[s * BLOCK : (s + 1) * BLOCK],
            VERY_LOW,
        )
        for s in range(SLOTS)
    ]
    top = masked[0]
    for part in masked[1:]:
        top = jnp.maximum(top, part)
    top = jnp.max(top, axis=0, keepdims=True)
    expos = [jnp.exp2((part - top) * (SCALE * math.log2(math.e))) for part in masked]
    total = expos[0]
    for part in expos[1:]:
        total = total + part
    inverse = 1.0 / jnp.sum(total, axis=0, keepdims=True)
    return jnp.concatenate([(part * inverse).astype(bf16) for part in expos], 0)


def pair_dweights(load_ref, qkv_ref, grads, pair):
    values = listed_pair(qkv_ref, load_ref, 2 * pair, 2)
    return lax.dot_general(values, side_by_side(grads), NT, preferred_element_type=f32)


def pair_dscores(weights_t, dweights, grads, outs):
    delta = jnp.sum((grads.astype(f32) * outs.astype(f32)).T, axis=0, keepdims=True)
    return (weights_t.astype(f32) * (dweights - delta)).astype(bf16)


def staggered(number, stages):
    for step in range(number + len(stages) - 1):
        for k in range(len(stages)):
            if 0 <= step - k < number:
                stages[k](step - k)


SCALARS = pl.BlockSpec(memory_space=pltpu.SMEM)
IN_VMEM = pl.BlockSpec(memory_space=pltpu.VMEM)


def resident(shape):
    zeros = (0,) * len(shape)
    return pl.BlockSpec(shape, lambda step: zeros, pipeline_mode=pl.Buffered(1))


def per_step(shape):
    zeros = (0,) * (len(shape) - 1)
    return pl.BlockSpec((PAIRS_PER_STEP,) + shape[1:], lambda step: (step,) + zeros)


def head_forward(qkv, tables):
    load, _, residue, offsets = tables
    pairs = residue.shape[0]
    weights_shape = (pairs, SLOTS * BLOCK, PAIR)
    out_shape = (pairs, PAIR, HEAD_DIM)

    def body(load_ref, residue_ref, offsets_ref, qkv_ref, weights_ref, o_ref):
        first = pl.program_id(0) * PAIRS_PER_STEP
        held = {}

        def scores(u):
            held[u] = pair_scores(load_ref, qkv_ref, first + u)

        def softmax(u):
            held[u] = pair_weights(residue_ref, offsets_ref, held[u], first + u)
            weights_ref[u] = held[u]

        def attend(u):
            out = rows_of_pair(held.pop(u), qkv_ref, load_ref, first + u, 2)
            o_ref[u] = out.astype(bf16)

        staggered(PAIRS_PER_STEP, (scores, softmax, attend))

    return pl.pallas_call(
        body,
        grid=(pairs // PAIRS_PER_STEP,),
        in_specs=[SCALARS, resident(residue.shape), resident(offsets.shape), IN_VMEM],
        out_specs=[
            per_step(weights_shape),
            per_step(out_shape),
        ],
        out_shape=[
            pltpu.HBM(weights_shape, bf16),
            pltpu.HBM(out_shape, bf16),
        ],
        cost_estimate=pl.CostEstimate(
            flops=20_000_000_000, transcendentals=3_000_000, bytes_accessed=10_000_000
        ),
        compiler_params=pltpu.CompilerParams(vmem_limit_bytes=VMEM_LIMIT),
        name="head_forward",
    )(load, residue, offsets, qkv)


def head_backward(qkv, g, o, weights, tables):
    load, store, _, _ = tables
    pairs = g.shape[0]
    blocks = 2 * pairs
    grads_shape = (pairs, 3, PAIR, HEAD_DIM)

    def body(
        load_ref, store_ref, weights_ref, qkv_ref, g_ref, o_ref, grads_ref, k_sum, v_sum
    ):
        @pl.when(pl.program_id(0) == 0)
        def _():
            k_sum[...] = jnp.zeros(k_sum.shape, f32)
            v_sum[...] = jnp.zeros(v_sum.shape, f32)

        first = pl.program_id(0) * PAIRS_PER_STEP
        held = {}

        def dweights(u):
            held[u] = pair_dweights(load_ref, qkv_ref, g_ref[u], first + u)

        def dscores(u):
            grads = g_ref[u]
            weights_t = weights_ref[u]
            held[u] = pair_dscores(weights_t, held[u], grads, o_ref[u])
            parts = lax.dot_general(
                weights_t, side_by_side(grads), NN, preferred_element_type=f32
            )
            add_to_listed(v_sum, parts, store_ref, 2 * (first + u))

        def dqk(u):
            q_diag = side_by_side(pair_queries(qkv_ref, first + u))
            parts = lax.dot_general(held[u], q_diag, NN, preferred_element_type=f32)
            add_to_listed(k_sum, parts, store_ref, 2 * (first + u))
            out = rows_of_pair(held.pop(u), qkv_ref, load_ref, first + u, 1)
            grads_ref[first + u, 0] = (out * SCALE).astype(bf16)

        staggered(PAIRS_PER_STEP, (dweights, dscores, dqk))

        @pl.when(pl.program_id(0) == pl.num_programs(0) - 1)
        def _():
            by_pair = (pairs, PAIR, HEAD_DIM)
            grads_ref[:, 1] = (k_sum[:blocks] * SCALE).astype(bf16).reshape(by_pair)
            grads_ref[:, 2] = v_sum[:blocks].astype(bf16).reshape(by_pair)

    return pl.pallas_call(
        body,
        grid=(pairs // PAIRS_PER_STEP,),
        in_specs=[
            SCALARS,
            SCALARS,
            per_step(weights.shape),
            IN_VMEM,
            per_step(g.shape),
            per_step(o.shape),
        ],
        out_specs=resident(grads_shape),
        out_shape=jax.ShapeDtypeStruct(grads_shape, bf16),
        scratch_shapes=[pltpu.VMEM((blocks + 1, BLOCK, HEAD_DIM), f32)] * 2,
        cost_estimate=pl.CostEstimate(
            flops=24_000_000_000, transcendentals=0, bytes_accessed=16_000_000
        ),
        compiler_params=pltpu.CompilerParams(vmem_limit_bytes=VMEM_LIMIT),
        name="head_backward",
    )(load, store, in_hbm(weights), qkv, in_hbm(g), in_hbm(o))


def exchange(by_device):
    return lax.all_to_all(by_device, "seq", split_axis=0, concat_axis=0, tiled=True)


def in_hbm(array):
    return pltpu.with_memory_space_constraint(array, pltpu.HBM)


def pack_heads(*arrays):
    tokens, width = arrays[0].shape
    number = len(arrays)

    def body(*refs):
        for a in range(number):
            for h in range(HEADS_PER_STEP):
                refs[number][h, a] = refs[a][:, h * HEAD_DIM : (h + 1) * HEAD_DIM]

    return pl.pallas_call(
        body,
        grid=(width // HEAD_DIM // HEADS_PER_STEP,),
        in_specs=[pl.BlockSpec((tokens, HEADS_PER_STEP * HEAD_DIM), lambda step: (0, step))]
        * number,
        out_specs=pl.BlockSpec(
            (HEADS_PER_STEP, number, tokens, HEAD_DIM), lambda step: (step, 0, 0, 0)
        ),
        out_shape=pltpu.HBM((width // HEAD_DIM, number, tokens, HEAD_DIM), bf16),
        compiler_params=pltpu.CompilerParams(vmem_limit_bytes=24 << 20),
        name="pack_heads",
    )(*[in_hbm(x) for x in arrays])


def unpack_heads(packed):
    heads, number, tokens, _ = packed.shape

    def body(packed_ref, *out_refs):
        for a in range(number):
            for h in range(HEADS_PER_STEP):
                out_refs[a][:, h * HEAD_DIM : (h + 1) * HEAD_DIM] = packed_ref[h, a]

    return pl.pallas_call(
        body,
        grid=(heads // HEADS_PER_STEP,),
        in_specs=[
            pl.BlockSpec((HEADS_PER_STEP, number, tokens, HEAD_DIM), lambda step: (step, 0, 0, 0))
        ],
        out_specs=[pl.BlockSpec((tokens, HEADS_PER_STEP * HEAD_DIM), lambda step: (0, step))]
        * number,
        out_shape=[jax.ShapeDtypeStruct((tokens, heads * HEAD_DIM), bf16)] * number,
        compiler_params=pltpu.CompilerParams(vmem_limit_bytes=24 << 20),
        name="unpack_heads",
    )(packed)


def local(queries, keys, values, out_grad, key_blocks, dilation):
    my_head = lax.axis_index("seq")
    tables = index_tables(
        lax.dynamic_index_in_dim(key_blocks, my_head, 0, keepdims=False),
        lax.dynamic_index_in_dim(dilation, my_head, 0, keepdims=False),
    )
    qkv = exchange(pack_heads(queries, keys, values)).reshape(-1, BLOCK, HEAD_DIM)
    packed_grad, tables = lax.optimization_barrier((pack_heads(out_grad), tables))
    g = exchange(packed_grad).reshape(-1, PAIR, HEAD_DIM)
    weights, o = head_forward(qkv, tables)
    attended = exchange(o[:, None])
    grads = exchange(head_backward(qkv, g, o, weights, tables))
    return tuple(unpack_heads(in_hbm(attended))) + tuple(unpack_heads(grads))


def solution(mesh):
    rows = P(("batch", "seq"), None)
    return jax.shard_map(
        local,
        mesh=mesh,
        in_specs=(rows, rows, rows, rows, P("batch", None, None), P("batch")),
        out_specs=(rows, rows, rows, rows),
        check_vma=False,
    )
```

```python
import functools
import math

import jax
import jax.numpy as jnp
from jax import lax
from jax.experimental import pallas as pl
from jax.experimental.pallas import tpu as pltpu
from jax.sharding import PartitionSpec as P

HEADS = 32
HEAD_DIM = 128
BLOCK = 64
PAIR = 2 * BLOCK
SLOTS = 12
SCALE = 1.0 / math.sqrt(HEAD_DIM)
VERY_LOW = -1e30
PAIRS_PER_STEP = 8
HEADS_PER_STEP = 16
VMEM_LIMIT = 30 << 20

f32 = jnp.float32
bf16 = jnp.bfloat16
NT = (((1,), (1,)), ((), ()))
NN = (((1,), (0,)), ((), ()))


def index_tables(lists, spacing):
    blocks = lists.shape[0]
    ids = jnp.arange(blocks, dtype=jnp.int32)[:, None]
    valid = lists >= 0
    listed_block = jnp.maximum(lists, 0)
    store = jnp.where(valid, lists, blocks)
    residue = jnp.where(valid, jnp.mod((listed_block - ids) * BLOCK, spacing), -1)
    residue = residue.reshape(blocks // 2, 2, SLOTS).transpose(0, 2, 1)
    residue = jnp.broadcast_to(residue[:, :, :, None], (blocks // 2, SLOTS, 2, BLOCK))
    residue = residue.reshape(blocks // 2, SLOTS, PAIR)
    residue = jnp.pad(residue, ((0, 0), (0, 16 - SLOTS), (0, 0)), constant_values=-1)
    key_at = lax.broadcasted_iota(jnp.int32, (BLOCK, PAIR), 0)
    query_at = lax.broadcasted_iota(jnp.int32, (BLOCK, PAIR), 1) % BLOCK
    offsets = jnp.mod(query_at - key_at, spacing)
    return listed_block, store, residue, jnp.stack([jnp.where(query_at >= key_at, offsets, -2), offsets])


def side_by_side(rows):
    zero = jnp.zeros((BLOCK, HEAD_DIM), rows.dtype)
    return jnp.concatenate(
        [
            jnp.concatenate([rows[:BLOCK], zero], 1),
            jnp.concatenate([zero, rows[BLOCK:]], 1),
        ],
        0,
    )


class Packed:
    def __init__(self, source, number, place):
        self.source, self.number, self.place = source, number, place

    def positions(self, blocks):
        return blocks // 2 * (2 * self.number) + 2 * self.place + blocks % 2


def listed(packed_ref, load_ref, block):
    return [packed_ref[load_ref[block, s]] for s in range(SLOTS)]


def listed_pair(packed_ref, load_ref, first):
    left = listed(packed_ref, load_ref, first)
    right = listed(packed_ref, load_ref, first + 1)
    return jnp.concatenate(
        [jnp.concatenate([a, b], 1) for a, b in zip(left, right)], 0
    )


def pair_queries(packed_ref, layout, pair):
    start = 2 * layout.number * pair + 2 * layout.place
    return packed_ref[pl.ds(start, 2)].reshape(PAIR, HEAD_DIM)


def rows_of_pair(weights_t, packed_ref, load_ref, pair):
    weights = weights_t.T
    outs = []
    for half in range(2):
        rows = jnp.concatenate(listed(packed_ref, load_ref, 2 * pair + half), 0)
        outs.append(
            lax.dot_general(
                weights[half * BLOCK : (half + 1) * BLOCK], rows, NN, preferred_element_type=f32
            )
        )
    return jnp.concatenate(outs, 0)


def add_to_listed(sum_ref, parts, store_ref, first, group=4):
    for half in range(2):
        for start in range(0, SLOTS, group):
            slots = range(start, start + group)
            blocks = [store_ref[first + half, s] for s in slots]
            before = [sum_ref[b] for b in blocks]
            for s, b, old in zip(slots, blocks, before):
                sum_ref[b] = (
                    old
                    + parts[
                        s * BLOCK : (s + 1) * BLOCK, half * HEAD_DIM : (half + 1) * HEAD_DIM
                    ]
                )


def pair_scores(load_ref, q_rows, keys_ref, pair):
    q_diag = side_by_side(q_rows)
    keys = listed_pair(keys_ref, load_ref, 2 * pair)
    return lax.dot_general(keys, q_diag, NT, preferred_element_type=f32)


def pair_weights(residue_ref, offsets_ref, scores, pair):
    residue = residue_ref[pair]
    masked = [
        jnp.where(
            offsets_ref[0 if s == 0 else 1] == residue[s : s + 1],
            scores[s * BLOCK : (s + 1) * BLOCK],
            VERY_LOW,
        )
        for s in range(SLOTS)
    ]
    top = masked[0]
    for part in masked[1:]:
        top = jnp.maximum(top, part)
    top = jnp.max(top, axis=0, keepdims=True)
    expos = [jnp.exp2((part - top) * (SCALE * math.log2(math.e))) for part in masked]
    total = expos[0]
    for part in expos[1:]:
        total = total + part
    inverse = 1.0 / jnp.sum(total, axis=0, keepdims=True)
    return jnp.concatenate([(part * inverse).astype(bf16) for part in expos], 0)


def pair_dweights(load_ref, values_ref, grads, pair):
    values = listed_pair(values_ref, load_ref, 2 * pair)
    return lax.dot_general(values, side_by_side(grads), NT, preferred_element_type=f32)


def pair_dscores(weights_t, dweights, grads, outs):
    delta = jnp.sum((grads.astype(f32) * outs.astype(f32)).T, axis=0, keepdims=True)
    return (weights_t.astype(f32) * (dweights - delta)).astype(bf16)


def staggered(number, stages):
    for step in range(number + len(stages) - 1):
        for k in range(len(stages)):
            if 0 <= step - k < number:
                stages[k](step - k)


SCALARS = pl.BlockSpec(memory_space=pltpu.SMEM)
IN_VMEM = pl.BlockSpec(memory_space=pltpu.VMEM)


def resident(shape):
    zeros = (0,) * len(shape)
    return pl.BlockSpec(shape, lambda step: zeros, pipeline_mode=pl.Buffered(1))


def per_step(shape):
    zeros = (0,) * (len(shape) - 1)
    return pl.BlockSpec((PAIRS_PER_STEP,) + shape[1:], lambda step: (step,) + zeros)


def head_forward(packed, layouts, tables):
    k_load, v_load, _, residue, offsets = tables
    q_at, k_at, v_at = layouts
    pairs = residue.shape[0]
    weights_shape = (pairs, SLOTS * BLOCK, PAIR)
    out_shape = (pairs, PAIR, HEAD_DIM)

    def body(k_load_ref, v_load_ref, residue_ref, offsets_ref, *refs):
        packed_refs, (weights_ref, o_ref) = refs[: len(packed)], refs[len(packed) :]
        k_ref, v_ref = packed_refs[k_at.source], packed_refs[v_at.source]
        first = pl.program_id(0) * PAIRS_PER_STEP
        held = {}

        def scores(u):
            q_rows = pair_queries(packed_refs[q_at.source], q_at, first + u)
            held[u] = pair_scores(k_load_ref, q_rows, k_ref, first + u)

        def softmax(u):
            held[u] = pair_weights(residue_ref, offsets_ref, held[u], first + u)
            weights_ref[u] = held[u]

        def attend(u):
            out = rows_of_pair(held.pop(u), v_ref, v_load_ref, first + u)
            o_ref[u] = out.astype(bf16)

        staggered(PAIRS_PER_STEP, (scores, softmax, attend))

    return pl.pallas_call(
        body,
        grid=(pairs // PAIRS_PER_STEP,),
        in_specs=[SCALARS, SCALARS, resident(residue.shape), resident(offsets.shape)]
        + [IN_VMEM] * len(packed),
        out_specs=[
            per_step(weights_shape),
            per_step(out_shape),
        ],
        out_shape=[
            pltpu.HBM(weights_shape, bf16),
            pltpu.HBM(out_shape, bf16),
        ],
        cost_estimate=pl.CostEstimate(
            flops=20_000_000_000, transcendentals=3_000_000, bytes_accessed=10_000_000
        ),
        compiler_params=pltpu.CompilerParams(vmem_limit_bytes=VMEM_LIMIT),
        name="head_forward",
    )(k_load, v_load, residue, offsets, *packed)


def head_backward(packed, layouts, g, o, weights, tables):
    k_load, v_load, store, _, _ = tables
    q_at, k_at, v_at = layouts
    pairs = g.shape[0]
    blocks = 2 * pairs
    grads_shape = (pairs, 3, PAIR, HEAD_DIM)

    def body(k_load_ref, v_load_ref, store_ref, weights_ref, g_ref, o_ref, *refs):
        packed_refs, (grads_ref, k_sum, v_sum) = refs[: len(packed)], refs[len(packed) :]
        k_ref, v_ref = packed_refs[k_at.source], packed_refs[v_at.source]

        @pl.when(pl.program_id(0) == 0)
        def _():
            k_sum[...] = jnp.zeros(k_sum.shape, f32)
            v_sum[...] = jnp.zeros(v_sum.shape, f32)

        first = pl.program_id(0) * PAIRS_PER_STEP
        held = {}

        def dweights(u):
            held[u] = pair_dweights(v_load_ref, v_ref, g_ref[u], first + u)

        def dscores(u):
            grads = g_ref[u]
            weights_t = weights_ref[u]
            held[u] = pair_dscores(weights_t, held[u], grads, o_ref[u])
            parts = lax.dot_general(
                weights_t, side_by_side(grads), NN, preferred_element_type=f32
            )
            add_to_listed(v_sum, parts, store_ref, 2 * (first + u))

        def dqk(u):
            q_rows = pair_queries(packed_refs[q_at.source], q_at, first + u)
            q_diag = side_by_side(q_rows)
            parts = lax.dot_general(held[u], q_diag, NN, preferred_element_type=f32)
            add_to_listed(k_sum, parts, store_ref, 2 * (first + u))
            out = rows_of_pair(held.pop(u), k_ref, k_load_ref, first + u)
            grads_ref[first + u, 0] = (out * SCALE).astype(bf16)

        staggered(PAIRS_PER_STEP, (dweights, dscores, dqk))

        @pl.when(pl.program_id(0) == pl.num_programs(0) - 1)
        def _():
            by_pair = (pairs, PAIR, HEAD_DIM)
            grads_ref[:, 1] = (k_sum[:blocks] * SCALE).astype(bf16).reshape(by_pair)
            grads_ref[:, 2] = v_sum[:blocks].astype(bf16).reshape(by_pair)

    return pl.pallas_call(
        body,
        grid=(pairs // PAIRS_PER_STEP,),
        in_specs=[
            SCALARS,
            SCALARS,
            SCALARS,
            per_step(weights.shape),
            per_step(g.shape),
            per_step(o.shape),
        ]
        + [IN_VMEM] * len(packed),
        out_specs=resident(grads_shape),
        out_shape=jax.ShapeDtypeStruct(grads_shape, bf16),
        scratch_shapes=[pltpu.VMEM((blocks + 1, BLOCK, HEAD_DIM), f32)] * 2,
        cost_estimate=pl.CostEstimate(
            flops=24_000_000_000, transcendentals=0, bytes_accessed=16_000_000
        ),
        compiler_params=pltpu.CompilerParams(vmem_limit_bytes=VMEM_LIMIT),
        name="head_backward",
    )(k_load, v_load, store, in_hbm(weights), in_hbm(g), in_hbm(o), *packed)


def exchange(by_device):
    return lax.all_to_all(by_device, "seq", split_axis=0, concat_axis=0, tiled=True)


def in_hbm(array):
    return pltpu.with_memory_space_constraint(array, pltpu.HBM)


def pack_heads(*arrays):
    tokens, width = arrays[0].shape
    number = len(arrays)

    def body(*refs):
        for a in range(number):
            for h in range(HEADS_PER_STEP):
                refs[number][h, a] = refs[a][:, h * HEAD_DIM : (h + 1) * HEAD_DIM]

    return pl.pallas_call(
        body,
        grid=(width // HEAD_DIM // HEADS_PER_STEP,),
        in_specs=[pl.BlockSpec((tokens, HEADS_PER_STEP * HEAD_DIM), lambda step: (0, step))]
        * number,
        out_specs=pl.BlockSpec(
            (HEADS_PER_STEP, number, tokens, HEAD_DIM), lambda step: (step, 0, 0, 0)
        ),
        out_shape=pltpu.HBM((width // HEAD_DIM, number, tokens, HEAD_DIM), bf16),
        compiler_params=pltpu.CompilerParams(vmem_limit_bytes=24 << 20),
        name="pack_heads",
    )(*[in_hbm(x) for x in arrays])


def unpack_heads(packed):
    heads, number, tokens, _ = packed.shape

    def body(packed_ref, *out_refs):
        for a in range(number):
            for h in range(HEADS_PER_STEP):
                out_refs[a][:, h * HEAD_DIM : (h + 1) * HEAD_DIM] = packed_ref[h, a]

    return pl.pallas_call(
        body,
        grid=(heads // HEADS_PER_STEP,),
        in_specs=[
            pl.BlockSpec((HEADS_PER_STEP, number, tokens, HEAD_DIM), lambda step: (step, 0, 0, 0))
        ],
        out_specs=[pl.BlockSpec((tokens, HEADS_PER_STEP * HEAD_DIM), lambda step: (0, step))]
        * number,
        out_shape=[jax.ShapeDtypeStruct((tokens, heads * HEAD_DIM), bf16)] * number,
        compiler_params=pltpu.CompilerParams(vmem_limit_bytes=24 << 20),
        name="unpack_heads",
    )(packed)


def after(first, *later):
    return lax.optimization_barrier((first,) + later)[1:]


def one_head(portions, layouts, queries, keys, values, out_grad, key_blocks, dilation):
    arrays = (queries, keys, values)
    packed = []
    for portion in portions:
        sources = [arrays[i] for i in portion]
        if packed:
            sources = after(packed[-1][:1, :1, :1, :1], *sources)
        packed.append(exchange(pack_heads(*sources)))
    packed = [x.reshape(-1, BLOCK, HEAD_DIM) for x in packed]
    my_head = lax.axis_index("seq")
    lists, store, residue, offsets = index_tables(
        lax.dynamic_index_in_dim(key_blocks, my_head, 0, keepdims=False),
        lax.dynamic_index_in_dim(dilation, my_head, 0, keepdims=False),
    )
    tables = (layouts[1].positions(lists), layouts[2].positions(lists), store, residue, offsets)
    packed_grad, tables = lax.optimization_barrier((pack_heads(out_grad), tables))
    g = exchange(packed_grad).reshape(-1, PAIR, HEAD_DIM)
    weights, o = head_forward(packed, layouts, tables)
    attended = exchange(o[:, None])
    grads = exchange(head_backward(packed, layouts, g, o, weights, tables))
    return tuple(unpack_heads(in_hbm(attended))) + tuple(unpack_heads(grads))


ALL_AT_ONCE = functools.partial(
    one_head, ((0, 1, 2),), (Packed(0, 3, 0), Packed(0, 3, 1), Packed(0, 3, 2))
)
VALUES_FIRST = functools.partial(
    one_head, ((2,), (0, 1)), (Packed(1, 2, 0), Packed(1, 2, 1), Packed(0, 1, 0))
)


def local(*arguments):
    odd = lax.axis_index("batch") % 2
    return lax.cond(odd == 0, ALL_AT_ONCE, VALUES_FIRST, *arguments)


def solution(mesh):
    rows = P(("batch", "seq"), None)
    return jax.shard_map(
        local,
        mesh=mesh,
        in_specs=(rows, rows, rows, rows, P("batch", None, None), P("batch")),
        out_specs=(rows, rows, rows, rows),
        check_vma=False,
    )
```

```python
import functools
import math

import jax
import jax.numpy as jnp
from jax import lax
from jax.experimental import pallas as pl
from jax.experimental.pallas import tpu as pltpu
from jax.sharding import PartitionSpec as P

HEADS = 32
HEAD_DIM = 128
BLOCK = 64
PAIR = 2 * BLOCK
SLOTS = 12
SCALE = 1.0 / math.sqrt(HEAD_DIM)
VERY_LOW = -1e30
PAIRS_PER_STEP = 8
PAIRS_AT_ONCE = 8
HEADS_PER_STEP = 16
VMEM_LIMIT = 30 << 20

f32 = jnp.float32
bf16 = jnp.bfloat16
NT = (((1,), (1,)), ((), ()))
NN = (((1,), (0,)), ((), ()))


def index_tables(lists, spacing):
    blocks = lists.shape[0]
    ids = jnp.arange(blocks, dtype=jnp.int32)[:, None]
    valid = lists >= 0
    listed_block = jnp.maximum(lists, 0)
    store = jnp.where(valid, lists, blocks)
    residue = jnp.where(valid, jnp.mod((listed_block - ids) * BLOCK, spacing), -1)
    residue = residue.reshape(blocks // 2, 2, SLOTS).transpose(0, 2, 1)
    residue = jnp.broadcast_to(residue[:, :, :, None], (blocks // 2, SLOTS, 2, BLOCK))
    residue = residue.reshape(blocks // 2, SLOTS, PAIR)
    residue = jnp.pad(residue, ((0, 0), (0, 16 - SLOTS), (0, 0)), constant_values=-1)
    key_at = lax.broadcasted_iota(jnp.int32, (BLOCK, PAIR), 0)
    query_at = lax.broadcasted_iota(jnp.int32, (BLOCK, PAIR), 1) % BLOCK
    offsets = jnp.mod(query_at - key_at, spacing)
    return listed_block, store, residue, jnp.stack([jnp.where(query_at >= key_at, offsets, -2), offsets])


def side_by_side(rows):
    zero = jnp.zeros((BLOCK, HEAD_DIM), rows.dtype)
    return jnp.concatenate(
        [
            jnp.concatenate([rows[:BLOCK], zero], 1),
            jnp.concatenate([zero, rows[BLOCK:]], 1),
        ],
        0,
    )


class Packed:
    def __init__(self, source, number, place):
        self.source, self.number, self.place = source, number, place

    def positions(self, blocks):
        return blocks // 2 * (2 * self.number) + 2 * self.place + blocks % 2


def listed(packed_ref, load_ref, block):
    return [packed_ref[load_ref[block, s]] for s in range(SLOTS)]


def listed_pair(packed_ref, load_ref, first):
    left = listed(packed_ref, load_ref, first)
    right = listed(packed_ref, load_ref, first + 1)
    return jnp.concatenate(
        [jnp.concatenate([a, b], 1) for a, b in zip(left, right)], 0
    )


def pair_queries(packed_ref, layout, pair):
    start = 2 * layout.number * pair + 2 * layout.place
    return packed_ref[pl.ds(start, 2)].reshape(PAIR, HEAD_DIM)


def rows_of_pair(weights_t, packed_ref, load_ref, pair):
    weights = weights_t.T
    outs = []
    for half in range(2):
        rows = jnp.concatenate(listed(packed_ref, load_ref, 2 * pair + half), 0)
        outs.append(
            lax.dot_general(
                weights[half * BLOCK : (half + 1) * BLOCK], rows, NN, preferred_element_type=f32
            )
        )
    return jnp.concatenate(outs, 0)


def add_to_listed(sum_ref, parts, store_ref, first, group=4):
    for half in range(2):
        for start in range(0, SLOTS, group):
            slots = range(start, start + group)
            blocks = [store_ref[first + half, s] for s in slots]
            before = [sum_ref[b] for b in blocks]
            for s, b, old in zip(slots, blocks, before):
                sum_ref[b] = (
                    old
                    + parts[
                        s * BLOCK : (s + 1) * BLOCK, half * HEAD_DIM : (half + 1) * HEAD_DIM
                    ]
                )


def pair_scores(load_ref, q_rows, keys_ref, pair):
    q_diag = side_by_side(q_rows)
    keys = listed_pair(keys_ref, load_ref, 2 * pair)
    return lax.dot_general(keys, q_diag, NT, preferred_element_type=f32)


def pair_weights(residue_ref, offsets_ref, scores, pair):
    residue = residue_ref[pair]
    masked = [
        jnp.where(
            offsets_ref[0 if s == 0 else 1] == residue[s : s + 1],
            scores[s * BLOCK : (s + 1) * BLOCK],
            VERY_LOW,
        )
        for s in range(SLOTS)
    ]
    top = masked[0]
    for part in masked[1:]:
        top = jnp.maximum(top, part)
    top = jnp.max(top, axis=0, keepdims=True)
    expos = [jnp.exp2((part - top) * (SCALE * math.log2(math.e))) for part in masked]
    total = expos[0]
    for part in expos[1:]:
        total = total + part
    inverse = 1.0 / jnp.sum(total, axis=0, keepdims=True)
    return jnp.concatenate([(part * inverse).astype(bf16) for part in expos], 0)


def pair_dweights(load_ref, values_ref, grads, pair):
    values = listed_pair(values_ref, load_ref, 2 * pair)
    return lax.dot_general(values, side_by_side(grads), NT, preferred_element_type=f32)


def pair_dscores(weights_t, dweights, grads, outs):
    delta = jnp.sum((grads.astype(f32) * outs.astype(f32)).T, axis=0, keepdims=True)
    return (weights_t.astype(f32) * (dweights - delta)).astype(bf16)


def staggered(number, stages):
    for step in range(number + len(stages) - 1):
        for k in range(len(stages)):
            if 0 <= step - k < number:
                stages[k](step - k)


SCALARS = pl.BlockSpec(memory_space=pltpu.SMEM)
IN_VMEM = pl.BlockSpec(memory_space=pltpu.VMEM)


def resident(shape):
    zeros = (0,) * len(shape)
    return pl.BlockSpec(shape, lambda step: zeros, pipeline_mode=pl.Buffered(1))


def per_step(shape):
    zeros = (0,) * (len(shape) - 1)
    return pl.BlockSpec((PAIRS_PER_STEP,) + shape[1:], lambda step: (step,) + zeros)


def head_forward(packed, layouts, tables):
    k_load, v_load, _, residue, offsets = tables
    q_at, k_at, v_at = layouts
    pairs = residue.shape[0]
    weights_shape = (pairs, SLOTS * BLOCK, PAIR)
    out_shape = (pairs, PAIR, HEAD_DIM)

    def body(k_load_ref, v_load_ref, residue_ref, offsets_ref, *refs):
        packed_refs, (weights_ref, o_ref) = refs[: len(packed)], refs[len(packed) :]
        k_ref, v_ref = packed_refs[k_at.source], packed_refs[v_at.source]
        first = pl.program_id(0) * PAIRS_PER_STEP
        held = {}

        def scores(u):
            q_rows = pair_queries(packed_refs[q_at.source], q_at, first + u)
            held[u] = pair_scores(k_load_ref, q_rows, k_ref, first + u)

        def softmax(u):
            held[u] = pair_weights(residue_ref, offsets_ref, held[u], first + u)
            weights_ref[u] = held[u]

        def attend(u):
            out = rows_of_pair(held.pop(u), v_ref, v_load_ref, first + u)
            o_ref[u] = out.astype(bf16)

        staggered(PAIRS_PER_STEP, (scores, softmax, attend))

    return pl.pallas_call(
        body,
        grid=(pairs // PAIRS_PER_STEP,),
        in_specs=[SCALARS, SCALARS, resident(residue.shape), resident(offsets.shape)]
        + [IN_VMEM] * len(packed),
        out_specs=[
            per_step(weights_shape),
            per_step(out_shape),
        ],
        out_shape=[
            pltpu.HBM(weights_shape, bf16),
            pltpu.HBM(out_shape, bf16),
        ],
        cost_estimate=pl.CostEstimate(
            flops=20_000_000_000, transcendentals=3_000_000, bytes_accessed=10_000_000
        ),
        compiler_params=pltpu.CompilerParams(vmem_limit_bytes=VMEM_LIMIT),
        name="head_forward",
    )(k_load, v_load, residue, offsets, *packed)


def head_backward(packed, layouts, g, o, weights, tables):
    k_load, v_load, store, _, _ = tables
    q_at, k_at, v_at = layouts
    pairs = g.shape[0]
    blocks = 2 * pairs
    grads_shape = (pairs, 3, PAIR, HEAD_DIM)

    def body(k_load_ref, v_load_ref, store_ref, weights_ref, g_ref, o_ref, *refs):
        packed_refs, (grads_ref, k_sum, v_sum) = refs[: len(packed)], refs[len(packed) :]
        k_ref, v_ref = packed_refs[k_at.source], packed_refs[v_at.source]

        @pl.when(pl.program_id(0) == 0)
        def _():
            k_sum[...] = jnp.zeros(k_sum.shape, f32)
            v_sum[...] = jnp.zeros(v_sum.shape, f32)

        first = pl.program_id(0) * PAIRS_PER_STEP
        held = {}

        def dweights(u):
            held[u] = pair_dweights(v_load_ref, v_ref, g_ref[u], first + u)

        def dscores(u):
            grads = g_ref[u]
            weights_t = weights_ref[u]
            held[u] = pair_dscores(weights_t, held[u], grads, o_ref[u])
            parts = lax.dot_general(
                weights_t, side_by_side(grads), NN, preferred_element_type=f32
            )
            add_to_listed(v_sum, parts, store_ref, 2 * (first + u))

        def dqk(u):
            q_rows = pair_queries(packed_refs[q_at.source], q_at, first + u)
            q_diag = side_by_side(q_rows)
            parts = lax.dot_general(held[u], q_diag, NN, preferred_element_type=f32)
            add_to_listed(k_sum, parts, store_ref, 2 * (first + u))
            out = rows_of_pair(held.pop(u), k_ref, k_load_ref, first + u)
            grads_ref[first + u, 0] = (out * SCALE).astype(bf16)

        staggered(PAIRS_PER_STEP, (dweights, dscores, dqk))

        @pl.when(pl.program_id(0) == pl.num_programs(0) - 1)
        def _():
            by_pair = (pairs, PAIR, HEAD_DIM)
            grads_ref[:, 1] = (k_sum[:blocks] * SCALE).astype(bf16).reshape(by_pair)
            grads_ref[:, 2] = v_sum[:blocks].astype(bf16).reshape(by_pair)

    return pl.pallas_call(
        body,
        grid=(pairs // PAIRS_PER_STEP,),
        in_specs=[
            SCALARS,
            SCALARS,
            SCALARS,
            per_step(weights.shape),
            per_step(g.shape),
            per_step(o.shape),
        ]
        + [IN_VMEM] * len(packed),
        out_specs=resident(grads_shape),
        out_shape=jax.ShapeDtypeStruct(grads_shape, bf16),
        scratch_shapes=[pltpu.VMEM((blocks + 1, BLOCK, HEAD_DIM), f32)] * 2,
        cost_estimate=pl.CostEstimate(
            flops=24_000_000_000, transcendentals=0, bytes_accessed=16_000_000
        ),
        compiler_params=pltpu.CompilerParams(vmem_limit_bytes=VMEM_LIMIT),
        name="head_backward",
    )(k_load, v_load, store, in_hbm(weights), in_hbm(g), in_hbm(o), *packed)


def head_at_once(packed, layouts, tables):
    k_load, v_load, store, residue, offsets = tables
    q_at, k_at, v_at, g_at = layouts
    pairs = residue.shape[0]
    blocks = 2 * pairs
    out_shape = (pairs, 4, PAIR, HEAD_DIM)

    def body(
        k_load_ref, v_load_ref, store_ref, residue_ref, offsets_ref, packed_ref, out_ref, k_sum, v_sum
    ):
        @pl.when(pl.program_id(0) == 0)
        def _():
            k_sum[...] = jnp.zeros(k_sum.shape, f32)
            v_sum[...] = jnp.zeros(v_sum.shape, f32)

        first = pl.program_id(0) * PAIRS_AT_ONCE
        held = {}
        weights = {}

        def scores(u):
            q_rows = pair_queries(packed_ref, q_at, first + u)
            held[u] = pair_scores(k_load_ref, q_rows, packed_ref, first + u)

        def softmax(u):
            weights[u] = pair_weights(residue_ref, offsets_ref, held[u], first + u)
            grads = pair_queries(packed_ref, g_at, first + u)
            held[u] = pair_dweights(v_load_ref, packed_ref, grads, first + u)

        def attend(u):
            out = rows_of_pair(weights[u], packed_ref, v_load_ref, first + u).astype(bf16)
            out_ref[first + u, 0] = out
            grads = pair_queries(packed_ref, g_at, first + u)
            held[u] = pair_dscores(weights[u], held[u], grads, out)

        def dvalues(u):
            grads = pair_queries(packed_ref, g_at, first + u)
            parts = lax.dot_general(
                weights.pop(u), side_by_side(grads), NN, preferred_element_type=f32
            )
            add_to_listed(v_sum, parts, store_ref, 2 * (first + u))

        def dqk(u):
            q_diag = side_by_side(pair_queries(packed_ref, q_at, first + u))
            parts = lax.dot_general(held[u], q_diag, NN, preferred_element_type=f32)
            add_to_listed(k_sum, parts, store_ref, 2 * (first + u))
            out = rows_of_pair(held.pop(u), packed_ref, k_load_ref, first + u)
            out_ref[first + u, 1] = (out * SCALE).astype(bf16)

        staggered(PAIRS_AT_ONCE, (scores, softmax, attend, dvalues, dqk))

        @pl.when(pl.program_id(0) == pl.num_programs(0) - 1)
        def _():
            by_pair = (pairs, PAIR, HEAD_DIM)
            out_ref[:, 2] = (k_sum[:blocks] * SCALE).astype(bf16).reshape(by_pair)
            out_ref[:, 3] = v_sum[:blocks].astype(bf16).reshape(by_pair)

    return pl.pallas_call(
        body,
        grid=(pairs // PAIRS_AT_ONCE,),
        in_specs=[SCALARS] * 3 + [resident(residue.shape), resident(offsets.shape), IN_VMEM],
        out_specs=resident(out_shape),
        out_shape=jax.ShapeDtypeStruct(out_shape, bf16),
        scratch_shapes=[pltpu.VMEM((blocks + 1, BLOCK, HEAD_DIM), f32)] * 2,
        cost_estimate=pl.CostEstimate(
            flops=44_000_000_000, transcendentals=3_000_000, bytes_accessed=10_000_000
        ),
        compiler_params=pltpu.CompilerParams(vmem_limit_bytes=VMEM_LIMIT),
        name="head_at_once",
    )(k_load, v_load, store, residue, offsets, packed)


def exchange(by_device):
    return lax.all_to_all(by_device, "seq", split_axis=0, concat_axis=0, tiled=True)


def in_hbm(array):
    return pltpu.with_memory_space_constraint(array, pltpu.HBM)


def pack_heads(*arrays):
    tokens, width = arrays[0].shape
    number = len(arrays)

    def body(*refs):
        for a in range(number):
            for h in range(HEADS_PER_STEP):
                refs[number][h, a] = refs[a][:, h * HEAD_DIM : (h + 1) * HEAD_DIM]

    return pl.pallas_call(
        body,
        grid=(width // HEAD_DIM // HEADS_PER_STEP,),
        in_specs=[pl.BlockSpec((tokens, HEADS_PER_STEP * HEAD_DIM), lambda step: (0, step))]
        * number,
        out_specs=pl.BlockSpec(
            (HEADS_PER_STEP, number, tokens, HEAD_DIM), lambda step: (step, 0, 0, 0)
        ),
        out_shape=pltpu.HBM((width // HEAD_DIM, number, tokens, HEAD_DIM), bf16),
        compiler_params=pltpu.CompilerParams(vmem_limit_bytes=24 << 20),
        name="pack_heads",
    )(*[in_hbm(x) for x in arrays])


def unpack_heads(packed):
    heads, number, tokens, _ = packed.shape

    def body(packed_ref, *out_refs):
        for a in range(number):
            for h in range(HEADS_PER_STEP):
                out_refs[a][:, h * HEAD_DIM : (h + 1) * HEAD_DIM] = packed_ref[h, a]

    return pl.pallas_call(
        body,
        grid=(heads // HEADS_PER_STEP,),
        in_specs=[
            pl.BlockSpec((HEADS_PER_STEP, number, tokens, HEAD_DIM), lambda step: (step, 0, 0, 0))
        ],
        out_specs=[pl.BlockSpec((tokens, HEADS_PER_STEP * HEAD_DIM), lambda step: (0, step))]
        * number,
        out_shape=[jax.ShapeDtypeStruct((tokens, heads * HEAD_DIM), bf16)] * number,
        compiler_params=pltpu.CompilerParams(vmem_limit_bytes=24 << 20),
        name="unpack_heads",
    )(packed)


def after(first, *later):
    return lax.optimization_barrier((first,) + later)[1:]


def one_head(portions, layouts, queries, keys, values, out_grad, key_blocks, dilation):
    arrays = (queries, keys, values)
    packed = []
    for portion in portions:
        sources = [arrays[i] for i in portion]
        if packed:
            sources = after(packed[-1][:1, :1, :1, :1], *sources)
        packed.append(exchange(pack_heads(*sources)))
    packed = [x.reshape(-1, BLOCK, HEAD_DIM) for x in packed]
    my_head = lax.axis_index("seq")
    lists, store, residue, offsets = index_tables(
        lax.dynamic_index_in_dim(key_blocks, my_head, 0, keepdims=False),
        lax.dynamic_index_in_dim(dilation, my_head, 0, keepdims=False),
    )
    tables = (layouts[1].positions(lists), layouts[2].positions(lists), store, residue, offsets)
    packed_grad, tables = lax.optimization_barrier((pack_heads(out_grad), tables))
    g = exchange(packed_grad).reshape(-1, PAIR, HEAD_DIM)
    weights, o = head_forward(packed, layouts, tables)
    attended = exchange(o[:, None])
    grads = exchange(head_backward(packed, layouts, g, o, weights, tables))
    return tuple(unpack_heads(in_hbm(attended))) + tuple(unpack_heads(grads))


def two_exchanges(queries, keys, values, out_grad, key_blocks, dilation):
    layouts = tuple(Packed(0, 4, i) for i in range(4))
    my_head = lax.axis_index("seq")
    lists, store, residue, offsets = index_tables(
        lax.dynamic_index_in_dim(key_blocks, my_head, 0, keepdims=False),
        lax.dynamic_index_in_dim(dilation, my_head, 0, keepdims=False),
    )
    tables = (layouts[1].positions(lists), layouts[2].positions(lists), store, residue, offsets)
    packed = exchange(pack_heads(queries, keys, values, out_grad)).reshape(-1, BLOCK, HEAD_DIM)
    return tuple(unpack_heads(exchange(head_at_once(packed, layouts, tables))))


ALL_AT_ONCE = functools.partial(
    one_head, ((0, 1, 2),), (Packed(0, 3, 0), Packed(0, 3, 1), Packed(0, 3, 2))
)
VALUES_FIRST = functools.partial(
    one_head, ((2,), (0, 1)), (Packed(1, 2, 0), Packed(1, 2, 1), Packed(0, 1, 0))
)


def local(*arguments):
    odd = lax.axis_index("batch") % 2
    return lax.cond(odd == 0, ALL_AT_ONCE, two_exchanges, *arguments)


def solution(mesh):
    rows = P(("batch", "seq"), None)
    return jax.shard_map(
        local,
        mesh=mesh,
        in_specs=(rows, rows, rows, rows, P("batch", None, None), P("batch")),
        out_specs=(rows, rows, rows, rows),
        check_vma=False,
    )
```

```python
import functools
import math

import jax
import jax.numpy as jnp
from jax import lax
from jax.experimental import pallas as pl
from jax.experimental.pallas import tpu as pltpu
from jax.sharding import PartitionSpec as P

HEADS = 32
HEAD_DIM = 128
BLOCK = 64
PAIR = 2 * BLOCK
SLOTS = 12
SCALE = 1.0 / math.sqrt(HEAD_DIM)
VERY_LOW = -1e30
PAIRS_PER_STEP = 8
PAIRS_AT_ONCE = 8
HEADS_PER_STEP = 16
VMEM_LIMIT = 30 << 20

f32 = jnp.float32
bf16 = jnp.bfloat16
NT = (((1,), (1,)), ((), ()))
NN = (((1,), (0,)), ((), ()))


def index_tables(lists, spacing):
    blocks = lists.shape[0]
    ids = jnp.arange(blocks, dtype=jnp.int32)[:, None]
    valid = lists >= 0
    listed_block = jnp.maximum(lists, 0)
    store = jnp.where(valid, lists, blocks)
    residue = jnp.where(valid, jnp.mod((listed_block - ids) * BLOCK, spacing), -1)
    residue = residue.reshape(blocks // 2, 2, SLOTS).transpose(0, 2, 1)
    residue = jnp.broadcast_to(residue[:, :, :, None], (blocks // 2, SLOTS, 2, BLOCK))
    residue = residue.reshape(blocks // 2, SLOTS, PAIR)
    residue = jnp.pad(residue, ((0, 0), (0, 16 - SLOTS), (0, 0)), constant_values=-1)
    key_at = lax.broadcasted_iota(jnp.int32, (BLOCK, PAIR), 0)
    query_at = lax.broadcasted_iota(jnp.int32, (BLOCK, PAIR), 1) % BLOCK
    offsets = jnp.mod(query_at - key_at, spacing)
    return listed_block, store, residue, jnp.stack([jnp.where(query_at >= key_at, offsets, -2), offsets])


def side_by_side(rows):
    zero = jnp.zeros((BLOCK, HEAD_DIM), rows.dtype)
    return jnp.concatenate(
        [
            jnp.concatenate([rows[:BLOCK], zero], 1),
            jnp.concatenate([zero, rows[BLOCK:]], 1),
        ],
        0,
    )


class Packed:
    def __init__(self, source, number, place):
        self.source, self.number, self.place = source, number, place

    def positions(self, blocks):
        return blocks // 2 * (2 * self.number) + 2 * self.place + blocks % 2


def listed(packed_ref, load_ref, block):
    return [packed_ref[load_ref[block, s]] for s in range(SLOTS)]


def listed_pair(packed_ref, load_ref, first):
    left = listed(packed_ref, load_ref, first)
    right = listed(packed_ref, load_ref, first + 1)
    return jnp.concatenate(
        [jnp.concatenate([a, b], 1) for a, b in zip(left, right)], 0
    )


def pair_queries(packed_ref, layout, pair):
    start = 2 * layout.number * pair + 2 * layout.place
    return packed_ref[pl.ds(start, 2)].reshape(PAIR, HEAD_DIM)


def rows_of_pair(weights_t, packed_ref, load_ref, pair):
    weights = weights_t.T
    outs = []
    for half in range(2):
        rows = jnp.concatenate(listed(packed_ref, load_ref, 2 * pair + half), 0)
        outs.append(
            lax.dot_general(
                weights[half * BLOCK : (half + 1) * BLOCK], rows, NN, preferred_element_type=f32
            )
        )
    return jnp.concatenate(outs, 0)


def add_to_listed(sum_ref, parts, store_ref, first, group=4):
    for half in range(2):
        for start in range(0, SLOTS, group):
            slots = range(start, start + group)
            blocks = [store_ref[first + half, s] for s in slots]
            before = [sum_ref[b] for b in blocks]
            for s, b, old in zip(slots, blocks, before):
                sum_ref[b] = (
                    old
                    + parts[
                        s * BLOCK : (s + 1) * BLOCK, half * HEAD_DIM : (half + 1) * HEAD_DIM
                    ]
                )


def pair_scores(load_ref, q_rows, keys_ref, pair):
    q_diag = side_by_side(q_rows)
    keys = listed_pair(keys_ref, load_ref, 2 * pair)
    return lax.dot_general(keys, q_diag, NT, preferred_element_type=f32)


def pair_weights(residue_ref, offsets_ref, scores, pair):
    residue = residue_ref[pair]
    masked = [
        jnp.where(
            offsets_ref[0 if s == 0 else 1] == residue[s : s + 1],
            scores[s * BLOCK : (s + 1) * BLOCK],
            VERY_LOW,
        )
        for s in range(SLOTS)
    ]
    top = masked[0]
    for part in masked[1:]:
        top = jnp.maximum(top, part)
    top = jnp.max(top, axis=0, keepdims=True)
    expos = [jnp.exp2((part - top) * (SCALE * math.log2(math.e))) for part in masked]
    total = expos[0]
    for part in expos[1:]:
        total = total + part
    inverse = 1.0 / jnp.sum(total, axis=0, keepdims=True)
    return jnp.concatenate([(part * inverse).astype(bf16) for part in expos], 0)


def pair_dweights(load_ref, values_ref, grads, pair):
    values = listed_pair(values_ref, load_ref, 2 * pair)
    return lax.dot_general(values, side_by_side(grads), NT, preferred_element_type=f32)


def pair_dscores(weights_t, dweights, grads, outs):
    delta = jnp.sum((grads.astype(f32) * outs.astype(f32)).T, axis=0, keepdims=True)
    return (weights_t.astype(f32) * (dweights - delta)).astype(bf16)


def staggered(number, stages):
    for step in range(number + len(stages) - 1):
        for k in range(len(stages)):
            if 0 <= step - k < number:
                stages[k](step - k)


SCALARS = pl.BlockSpec(memory_space=pltpu.SMEM)
IN_VMEM = pl.BlockSpec(memory_space=pltpu.VMEM)


def resident(shape):
    zeros = (0,) * len(shape)
    return pl.BlockSpec(shape, lambda step: zeros, pipeline_mode=pl.Buffered(1))


def per_step(shape):
    zeros = (0,) * (len(shape) - 1)
    return pl.BlockSpec((PAIRS_PER_STEP,) + shape[1:], lambda step: (step,) + zeros)


def head_forward(packed, layouts, tables):
    k_load, v_load, _, residue, offsets = tables
    q_at, k_at, v_at = layouts
    pairs = residue.shape[0]
    weights_shape = (pairs, SLOTS * BLOCK, PAIR)
    out_shape = (pairs, PAIR, HEAD_DIM)

    def body(k_load_ref, v_load_ref, residue_ref, offsets_ref, *refs):
        packed_refs, (weights_ref, o_ref) = refs[: len(packed)], refs[len(packed) :]
        k_ref, v_ref = packed_refs[k_at.source], packed_refs[v_at.source]
        first = pl.program_id(0) * PAIRS_PER_STEP
        held = {}

        def scores(u):
            q_rows = pair_queries(packed_refs[q_at.source], q_at, first + u)
            held[u] = pair_scores(k_load_ref, q_rows, k_ref, first + u)

        def softmax(u):
            held[u] = pair_weights(residue_ref, offsets_ref, held[u], first + u)
            weights_ref[u] = held[u]

        def attend(u):
            out = rows_of_pair(held.pop(u), v_ref, v_load_ref, first + u)
            o_ref[u] = out.astype(bf16)

        staggered(PAIRS_PER_STEP, (scores, softmax, attend))

    return pl.pallas_call(
        body,
        grid=(pairs // PAIRS_PER_STEP,),
        in_specs=[SCALARS, SCALARS, resident(residue.shape), resident(offsets.shape)]
        + [IN_VMEM] * len(packed),
        out_specs=[
            per_step(weights_shape),
            per_step(out_shape),
        ],
        out_shape=[
            pltpu.HBM(weights_shape, bf16),
            pltpu.HBM(out_shape, bf16),
        ],
        cost_estimate=pl.CostEstimate(
            flops=20_000_000_000, transcendentals=3_000_000, bytes_accessed=10_000_000
        ),
        compiler_params=pltpu.CompilerParams(vmem_limit_bytes=VMEM_LIMIT),
        name="head_forward",
    )(k_load, v_load, residue, offsets, *packed)


def send_step(stage_ref, out_ref, sems, pairs, arrays):
    step = pl.program_id(0)
    part = (pl.ds(step * pairs, pairs), pl.ds(0, arrays))
    pltpu.make_async_copy(stage_ref.at[part], out_ref.at[part], sems.at[step]).start()


def send_sums(stage_ref, out_ref, sems, steps, pairs, arrays, k_sum, v_sum):
    copies = []
    for step in range(steps):
        part = (pl.ds(step * pairs, pairs), pl.ds(0, arrays))
        copies.append(pltpu.make_async_copy(stage_ref.at[part], out_ref.at[part], sems.at[step]))
    for step in range(steps):
        rows = pl.ds(step * pairs, pairs)
        blocks = pl.ds(2 * step * pairs, 2 * pairs)
        by_pair = (pairs, PAIR, HEAD_DIM)
        stage_ref[rows, arrays] = (k_sum[blocks] * SCALE).astype(bf16).reshape(by_pair)
        stage_ref[rows, arrays + 1] = v_sum[blocks].astype(bf16).reshape(by_pair)
        part = (rows, pl.ds(arrays, 2))
        copy = pltpu.make_async_copy(stage_ref.at[part], out_ref.at[part], sems.at[steps + step])
        copy.start()
        copies.append(copy)
    for copy in copies:
        copy.wait()


def head_backward(packed, layouts, g, o, weights, tables):
    k_load, v_load, store, _, _ = tables
    q_at, k_at, v_at = layouts
    pairs = g.shape[0]
    blocks = 2 * pairs
    grads_shape = (pairs, 3, PAIR, HEAD_DIM)
    steps = pairs // PAIRS_PER_STEP

    def body(k_load_ref, v_load_ref, store_ref, weights_ref, g_ref, o_ref, *refs):
        packed_refs = refs[: len(packed)]
        out_ref, k_sum, v_sum, grads_ref, sems = refs[len(packed) :]
        k_ref, v_ref = packed_refs[k_at.source], packed_refs[v_at.source]

        @pl.when(pl.program_id(0) == 0)
        def _():
            k_sum[...] = jnp.zeros(k_sum.shape, f32)
            v_sum[...] = jnp.zeros(v_sum.shape, f32)

        first = pl.program_id(0) * PAIRS_PER_STEP
        held = {}

        def dweights(u):
            held[u] = pair_dweights(v_load_ref, v_ref, g_ref[u], first + u)

        def dscores(u):
            grads = g_ref[u]
            weights_t = weights_ref[u]
            held[u] = pair_dscores(weights_t, held[u], grads, o_ref[u])
            parts = lax.dot_general(
                weights_t, side_by_side(grads), NN, preferred_element_type=f32
            )
            add_to_listed(v_sum, parts, store_ref, 2 * (first + u))

        def dqk(u):
            q_rows = pair_queries(packed_refs[q_at.source], q_at, first + u)
            q_diag = side_by_side(q_rows)
            parts = lax.dot_general(held[u], q_diag, NN, preferred_element_type=f32)
            add_to_listed(k_sum, parts, store_ref, 2 * (first + u))
            out = rows_of_pair(held.pop(u), k_ref, k_load_ref, first + u)
            grads_ref[first + u, 0] = (out * SCALE).astype(bf16)

        staggered(PAIRS_PER_STEP, (dweights, dscores, dqk))
        send_step(grads_ref, out_ref, sems, PAIRS_PER_STEP, 1)

        @pl.when(pl.program_id(0) == steps - 1)
        def _():
            send_sums(grads_ref, out_ref, sems, steps, PAIRS_PER_STEP, 1, k_sum, v_sum)

    return pl.pallas_call(
        body,
        grid=(pairs // PAIRS_PER_STEP,),
        in_specs=[
            SCALARS,
            SCALARS,
            SCALARS,
            per_step(weights.shape),
            per_step(g.shape),
            per_step(o.shape),
        ]
        + [IN_VMEM] * len(packed),
        out_specs=pl.BlockSpec(memory_space=pltpu.HBM),
        out_shape=pltpu.HBM(grads_shape, bf16),
        scratch_shapes=[pltpu.VMEM((blocks + 1, BLOCK, HEAD_DIM), f32)] * 2
        + [pltpu.VMEM(grads_shape, bf16), pltpu.SemaphoreType.DMA((2 * steps,))],
        cost_estimate=pl.CostEstimate(
            flops=24_000_000_000, transcendentals=0, bytes_accessed=16_000_000
        ),
        compiler_params=pltpu.CompilerParams(vmem_limit_bytes=VMEM_LIMIT),
        name="head_backward",
    )(k_load, v_load, store, in_hbm(weights), in_hbm(g), in_hbm(o), *packed)


def head_at_once(packed, layouts, tables):
    k_load, v_load, store, residue, offsets = tables
    q_at, k_at, v_at, g_at = layouts
    pairs = residue.shape[0]
    blocks = 2 * pairs
    out_shape = (pairs, 4, PAIR, HEAD_DIM)
    steps = pairs // PAIRS_AT_ONCE

    def body(
        k_load_ref, v_load_ref, store_ref, residue_ref, offsets_ref, packed_ref, sent_ref,
        k_sum, v_sum, out_ref, sems,
    ):
        @pl.when(pl.program_id(0) == 0)
        def _():
            k_sum[...] = jnp.zeros(k_sum.shape, f32)
            v_sum[...] = jnp.zeros(v_sum.shape, f32)

        first = pl.program_id(0) * PAIRS_AT_ONCE
        held = {}
        weights = {}

        def scores(u):
            q_rows = pair_queries(packed_ref, q_at, first + u)
            held[u] = pair_scores(k_load_ref, q_rows, packed_ref, first + u)

        def softmax(u):
            weights[u] = pair_weights(residue_ref, offsets_ref, held[u], first + u)
            grads = pair_queries(packed_ref, g_at, first + u)
            held[u] = pair_dweights(v_load_ref, packed_ref, grads, first + u)

        def attend(u):
            out = rows_of_pair(weights[u], packed_ref, v_load_ref, first + u).astype(bf16)
            out_ref[first + u, 0] = out
            grads = pair_queries(packed_ref, g_at, first + u)
            held[u] = pair_dscores(weights[u], held[u], grads, out)

        def dvalues(u):
            grads = pair_queries(packed_ref, g_at, first + u)
            parts = lax.dot_general(
                weights.pop(u), side_by_side(grads), NN, preferred_element_type=f32
            )
            add_to_listed(v_sum, parts, store_ref, 2 * (first + u))

        def dqk(u):
            q_diag = side_by_side(pair_queries(packed_ref, q_at, first + u))
            parts = lax.dot_general(held[u], q_diag, NN, preferred_element_type=f32)
            add_to_listed(k_sum, parts, store_ref, 2 * (first + u))
            out = rows_of_pair(held.pop(u), packed_ref, k_load_ref, first + u)
            out_ref[first + u, 1] = (out * SCALE).astype(bf16)

        staggered(PAIRS_AT_ONCE, (scores, softmax, attend, dvalues, dqk))
        send_step(out_ref, sent_ref, sems, PAIRS_AT_ONCE, 2)

        @pl.when(pl.program_id(0) == steps - 1)
        def _():
            send_sums(out_ref, sent_ref, sems, steps, PAIRS_AT_ONCE, 2, k_sum, v_sum)

    return pl.pallas_call(
        body,
        grid=(pairs // PAIRS_AT_ONCE,),
        in_specs=[SCALARS] * 3 + [resident(residue.shape), resident(offsets.shape), IN_VMEM],
        out_specs=pl.BlockSpec(memory_space=pltpu.HBM),
        out_shape=pltpu.HBM(out_shape, bf16),
        scratch_shapes=[pltpu.VMEM((blocks + 1, BLOCK, HEAD_DIM), f32)] * 2
        + [pltpu.VMEM(out_shape, bf16), pltpu.SemaphoreType.DMA((2 * steps,))],
        cost_estimate=pl.CostEstimate(
            flops=44_000_000_000, transcendentals=3_000_000, bytes_accessed=10_000_000
        ),
        compiler_params=pltpu.CompilerParams(vmem_limit_bytes=VMEM_LIMIT),
        name="head_at_once",
    )(k_load, v_load, store, residue, offsets, packed)


def exchange(by_device):
    return lax.all_to_all(by_device, "seq", split_axis=0, concat_axis=0, tiled=True)


def in_hbm(array):
    return pltpu.with_memory_space_constraint(array, pltpu.HBM)


def pack_heads(*arrays):
    tokens, width = arrays[0].shape
    number = len(arrays)

    def body(*refs):
        for a in range(number):
            for h in range(HEADS_PER_STEP):
                refs[number][h, a] = refs[a][:, h * HEAD_DIM : (h + 1) * HEAD_DIM]

    return pl.pallas_call(
        body,
        grid=(width // HEAD_DIM // HEADS_PER_STEP,),
        in_specs=[pl.BlockSpec((tokens, HEADS_PER_STEP * HEAD_DIM), lambda step: (0, step))]
        * number,
        out_specs=pl.BlockSpec(
            (HEADS_PER_STEP, number, tokens, HEAD_DIM), lambda step: (step, 0, 0, 0)
        ),
        out_shape=pltpu.HBM((width // HEAD_DIM, number, tokens, HEAD_DIM), bf16),
        compiler_params=pltpu.CompilerParams(vmem_limit_bytes=24 << 20),
        name="pack_heads",
    )(*[in_hbm(x) for x in arrays])


def unpack_heads(packed):
    heads, number, tokens, _ = packed.shape

    def body(packed_ref, *out_refs):
        for a in range(number):
            for h in range(HEADS_PER_STEP):
                out_refs[a][:, h * HEAD_DIM : (h + 1) * HEAD_DIM] = packed_ref[h, a]

    return pl.pallas_call(
        body,
        grid=(heads // HEADS_PER_STEP,),
        in_specs=[
            pl.BlockSpec((HEADS_PER_STEP, number, tokens, HEAD_DIM), lambda step: (step, 0, 0, 0))
        ],
        out_specs=[pl.BlockSpec((tokens, HEADS_PER_STEP * HEAD_DIM), lambda step: (0, step))]
        * number,
        out_shape=[jax.ShapeDtypeStruct((tokens, heads * HEAD_DIM), bf16)] * number,
        compiler_params=pltpu.CompilerParams(vmem_limit_bytes=24 << 20),
        name="unpack_heads",
    )(packed)


def after(first, *later):
    return lax.optimization_barrier((first,) + later)[1:]


def one_head(portions, layouts, queries, keys, values, out_grad, key_blocks, dilation):
    arrays = (queries, keys, values)
    packed = []
    for portion in portions:
        sources = [arrays[i] for i in portion]
        if packed:
            sources = after(packed[-1][:1, :1, :1, :1], *sources)
        packed.append(exchange(pack_heads(*sources)))
    packed = [x.reshape(-1, BLOCK, HEAD_DIM) for x in packed]
    my_head = lax.axis_index("seq")
    lists, store, residue, offsets = index_tables(
        lax.dynamic_index_in_dim(key_blocks, my_head, 0, keepdims=False),
        lax.dynamic_index_in_dim(dilation, my_head, 0, keepdims=False),
    )
    tables = (layouts[1].positions(lists), layouts[2].positions(lists), store, residue, offsets)
    tables = tuple(in_hbm(x) for x in tables)
    packed_grad, tables = lax.optimization_barrier((pack_heads(out_grad), tables))
    g = exchange(packed_grad).reshape(-1, PAIR, HEAD_DIM)
    weights, o = head_forward(packed, layouts, tables)
    attended = exchange(o[:, None])
    grads = exchange(head_backward(packed, layouts, g, o, weights, tables))
    return tuple(unpack_heads(in_hbm(attended))) + tuple(unpack_heads(grads))


def two_exchanges(queries, keys, values, out_grad, key_blocks, dilation):
    layouts = tuple(Packed(0, 4, i) for i in range(4))
    my_head = lax.axis_index("seq")
    lists, store, residue, offsets = index_tables(
        lax.dynamic_index_in_dim(key_blocks, my_head, 0, keepdims=False),
        lax.dynamic_index_in_dim(dilation, my_head, 0, keepdims=False),
    )
    tables = (layouts[1].positions(lists), layouts[2].positions(lists), store, residue, offsets)
    packed = exchange(pack_heads(queries, keys, values, out_grad)).reshape(-1, BLOCK, HEAD_DIM)
    return tuple(unpack_heads(exchange(head_at_once(packed, layouts, tables))))


ALL_AT_ONCE = functools.partial(
    one_head, ((0, 1, 2),), (Packed(0, 3, 0), Packed(0, 3, 1), Packed(0, 3, 2))
)
VALUES_FIRST = functools.partial(
    one_head, ((2,), (0, 1)), (Packed(1, 2, 0), Packed(1, 2, 1), Packed(0, 1, 0))
)


def local(*arguments):
    odd = lax.axis_index("batch") % 2
    return lax.cond(odd == 0, ALL_AT_ONCE, two_exchanges, *arguments)


def solution(mesh):
    rows = P(("batch", "seq"), None)
    return jax.shard_map(
        local,
        mesh=mesh,
        in_specs=(rows, rows, rows, rows, P("batch", None, None), P("batch")),
        out_specs=(rows, rows, rows, rows),
        check_vma=False,
    )
```

```python
import functools
import math

import jax
import jax.numpy as jnp
from jax import lax
from jax.experimental import pallas as pl
from jax.experimental.pallas import tpu as pltpu
from jax.sharding import PartitionSpec as P

HEADS = 32
HEAD_DIM = 128
BLOCK = 64
PAIR = 2 * BLOCK
SLOTS = 12
SCALE = 1.0 / math.sqrt(HEAD_DIM)
VERY_LOW = -1e30
PAIRS_PER_STEP = 8
PAIRS_AT_ONCE = 8
HEADS_PER_STEP = 16
VMEM_LIMIT = 30 << 20

f32 = jnp.float32
bf16 = jnp.bfloat16
NT = (((1,), (1,)), ((), ()))
NN = (((1,), (0,)), ((), ()))


def index_tables(lists, spacing):
    blocks = lists.shape[0]
    ids = jnp.arange(blocks, dtype=jnp.int32)[:, None]
    valid = lists >= 0
    listed_block = jnp.maximum(lists, 0)
    store = jnp.where(valid, lists, blocks)
    residue = jnp.where(valid, jnp.mod((listed_block - ids) * BLOCK, spacing), -1)
    residue = residue.reshape(blocks // 2, 2, SLOTS).transpose(0, 2, 1)
    residue = jnp.broadcast_to(residue[:, :, :, None], (blocks // 2, SLOTS, 2, BLOCK))
    residue = residue.reshape(blocks // 2, SLOTS, PAIR)
    residue = jnp.pad(residue, ((0, 0), (0, 16 - SLOTS), (0, 0)), constant_values=-1)
    key_at = lax.broadcasted_iota(jnp.int32, (BLOCK, PAIR), 0)
    query_at = lax.broadcasted_iota(jnp.int32, (BLOCK, PAIR), 1) % BLOCK
    offsets = jnp.mod(query_at - key_at, spacing)
    return listed_block, store, residue, jnp.stack([jnp.where(query_at >= key_at, offsets, -2), offsets])


def side_by_side(rows):
    zero = jnp.zeros((BLOCK, HEAD_DIM), rows.dtype)
    return jnp.concatenate(
        [
            jnp.concatenate([rows[:BLOCK], zero], 1),
            jnp.concatenate([zero, rows[BLOCK:]], 1),
        ],
        0,
    )


class Packed:
    def __init__(self, source, number, place):
        self.source, self.number, self.place = source, number, place

    def positions(self, blocks):
        return blocks // 2 * (2 * self.number) + 2 * self.place + blocks % 2


def listed(packed_ref, load_ref, block):
    return [packed_ref[load_ref[block, s]] for s in range(SLOTS)]


def listed_pair(packed_ref, load_ref, first):
    left = listed(packed_ref, load_ref, first)
    right = listed(packed_ref, load_ref, first + 1)
    return jnp.concatenate(
        [jnp.concatenate([a, b], 1) for a, b in zip(left, right)], 0
    )


def pair_queries(packed_ref, layout, pair):
    start = 2 * layout.number * pair + 2 * layout.place
    return packed_ref[pl.ds(start, 2)].reshape(PAIR, HEAD_DIM)


def rows_of_pair(weights_t, packed_ref, load_ref, pair):
    weights = weights_t.T
    outs = []
    for half in range(2):
        rows = jnp.concatenate(listed(packed_ref, load_ref, 2 * pair + half), 0)
        outs.append(
            lax.dot_general(
                weights[half * BLOCK : (half + 1) * BLOCK], rows, NN, preferred_element_type=f32
            )
        )
    return jnp.concatenate(outs, 0)


def add_to_listed(sum_ref, parts, store_ref, first, group=4):
    for half in range(2):
        for start in range(0, SLOTS, group):
            slots = range(start, start + group)
            blocks = [store_ref[first + half, s] for s in slots]
            before = [sum_ref[b] for b in blocks]
            for s, b, old in zip(slots, blocks, before):
                sum_ref[b] = (
                    old
                    + parts[
                        s * BLOCK : (s + 1) * BLOCK, half * HEAD_DIM : (half + 1) * HEAD_DIM
                    ]
                )


def pair_scores(load_ref, q_rows, keys_ref, pair):
    q_diag = side_by_side(q_rows)
    keys = listed_pair(keys_ref, load_ref, 2 * pair)
    return lax.dot_general(keys, q_diag, NT, preferred_element_type=f32)


def pair_weights(residue_ref, offsets_ref, scores, pair):
    residue = residue_ref[pair]
    masked = [
        jnp.where(
            offsets_ref[0 if s == 0 else 1] == residue[s : s + 1],
            scores[s * BLOCK : (s + 1) * BLOCK],
            VERY_LOW,
        )
        for s in range(SLOTS)
    ]
    top = masked[0]
    for part in masked[1:]:
        top = jnp.maximum(top, part)
    top = jnp.max(top, axis=0, keepdims=True)
    expos = [jnp.exp2((part - top) * (SCALE * math.log2(math.e))) for part in masked]
    total = expos[0]
    for part in expos[1:]:
        total = total + part
    inverse = 1.0 / jnp.sum(total, axis=0, keepdims=True)
    return jnp.concatenate([(part * inverse).astype(bf16) for part in expos], 0)


def pair_dweights(load_ref, values_ref, grads, pair):
    values = listed_pair(values_ref, load_ref, 2 * pair)
    return lax.dot_general(values, side_by_side(grads), NT, preferred_element_type=f32)


def pair_dscores(weights_t, dweights, grads, outs):
    delta = jnp.sum((grads.astype(f32) * outs.astype(f32)).T, axis=0, keepdims=True)
    return (weights_t.astype(f32) * (dweights - delta)).astype(bf16)


def staggered(number, stages):
    for step in range(number + len(stages) - 1):
        for k in range(len(stages)):
            if 0 <= step - k < number:
                stages[k](step - k)


SCALARS = pl.BlockSpec(memory_space=pltpu.SMEM)
IN_VMEM = pl.BlockSpec(memory_space=pltpu.VMEM)


def resident(shape):
    zeros = (0,) * len(shape)
    return pl.BlockSpec(shape, lambda step: zeros, pipeline_mode=pl.Buffered(1))


def per_step(shape):
    zeros = (0,) * (len(shape) - 1)
    return pl.BlockSpec((PAIRS_PER_STEP,) + shape[1:], lambda step: (step,) + zeros)


def head_forward(packed, layouts, tables):
    k_load, v_load, _, residue, offsets = tables
    q_at, k_at, v_at = layouts
    pairs = residue.shape[0]
    weights_shape = (pairs, SLOTS * BLOCK, PAIR)
    out_shape = (pairs, PAIR, HEAD_DIM)

    def body(k_load_ref, v_load_ref, residue_ref, offsets_ref, *refs):
        packed_refs, (weights_ref, o_ref) = refs[: len(packed)], refs[len(packed) :]
        k_ref, v_ref = packed_refs[k_at.source], packed_refs[v_at.source]
        first = pl.program_id(0) * PAIRS_PER_STEP
        held = {}

        def scores(u):
            q_rows = pair_queries(packed_refs[q_at.source], q_at, first + u)
            held[u] = pair_scores(k_load_ref, q_rows, k_ref, first + u)

        def softmax(u):
            held[u] = pair_weights(residue_ref, offsets_ref, held[u], first + u)
            weights_ref[u] = held[u]

        def attend(u):
            out = rows_of_pair(held.pop(u), v_ref, v_load_ref, first + u)
            o_ref[u] = out.astype(bf16)

        staggered(PAIRS_PER_STEP, (scores, softmax, attend))

    return pl.pallas_call(
        body,
        grid=(pairs // PAIRS_PER_STEP,),
        in_specs=[SCALARS, SCALARS, resident(residue.shape), resident(offsets.shape)]
        + [IN_VMEM] * len(packed),
        out_specs=[
            per_step(weights_shape),
            per_step(out_shape),
        ],
        out_shape=[
            pltpu.HBM(weights_shape, bf16),
            pltpu.HBM(out_shape, bf16),
        ],
        cost_estimate=pl.CostEstimate(
            flops=20_000_000_000, transcendentals=3_000_000, bytes_accessed=10_000_000
        ),
        compiler_params=pltpu.CompilerParams(vmem_limit_bytes=VMEM_LIMIT),
        name="head_forward",
    )(k_load, v_load, residue, offsets, *packed)


def head_backward(packed, layouts, g, o, weights, tables):
    k_load, v_load, store, _, _ = tables
    q_at, k_at, v_at = layouts
    pairs = g.shape[0]
    blocks = 2 * pairs
    grads_shape = (pairs, 3, PAIR, HEAD_DIM)

    def body(k_load_ref, v_load_ref, store_ref, weights_ref, g_ref, o_ref, *refs):
        packed_refs, (grads_ref, k_sum, v_sum) = refs[: len(packed)], refs[len(packed) :]
        k_ref, v_ref = packed_refs[k_at.source], packed_refs[v_at.source]

        @pl.when(pl.program_id(0) == 0)
        def _():
            k_sum[...] = jnp.zeros(k_sum.shape, f32)
            v_sum[...] = jnp.zeros(v_sum.shape, f32)

        first = pl.program_id(0) * PAIRS_PER_STEP
        held = {}

        def dweights(u):
            held[u] = pair_dweights(v_load_ref, v_ref, g_ref[u], first + u)

        def dscores(u):
            grads = g_ref[u]
            weights_t = weights_ref[u]
            held[u] = pair_dscores(weights_t, held[u], grads, o_ref[u])
            parts = lax.dot_general(
                weights_t, side_by_side(grads), NN, preferred_element_type=f32
            )
            add_to_listed(v_sum, parts, store_ref, 2 * (first + u))

        def dqk(u):
            q_rows = pair_queries(packed_refs[q_at.source], q_at, first + u)
            q_diag = side_by_side(q_rows)
            parts = lax.dot_general(held[u], q_diag, NN, preferred_element_type=f32)
            add_to_listed(k_sum, parts, store_ref, 2 * (first + u))
            out = rows_of_pair(held.pop(u), k_ref, k_load_ref, first + u)
            grads_ref[first + u, 0] = (out * SCALE).astype(bf16)

        staggered(PAIRS_PER_STEP, (dweights, dscores, dqk))

        @pl.when(pl.program_id(0) == pl.num_programs(0) - 1)
        def _():
            by_pair = (pairs, PAIR, HEAD_DIM)
            grads_ref[:, 1] = (k_sum[:blocks] * SCALE).astype(bf16).reshape(by_pair)
            grads_ref[:, 2] = v_sum[:blocks].astype(bf16).reshape(by_pair)

    return pl.pallas_call(
        body,
        grid=(pairs // PAIRS_PER_STEP,),
        in_specs=[
            SCALARS,
            SCALARS,
            SCALARS,
            per_step(weights.shape),
            per_step(g.shape),
            per_step(o.shape),
        ]
        + [IN_VMEM] * len(packed),
        out_specs=resident(grads_shape),
        out_shape=jax.ShapeDtypeStruct(grads_shape, bf16),
        scratch_shapes=[pltpu.VMEM((blocks + 1, BLOCK, HEAD_DIM), f32)] * 2,
        cost_estimate=pl.CostEstimate(
            flops=24_000_000_000, transcendentals=0, bytes_accessed=16_000_000
        ),
        compiler_params=pltpu.CompilerParams(vmem_limit_bytes=VMEM_LIMIT),
        name="head_backward",
    )(k_load, v_load, store, in_hbm(weights), in_hbm(g), in_hbm(o), *packed)


def head_at_once(packed, layouts, tables):
    k_load, v_load, store, residue, offsets = tables
    q_at, k_at, v_at, g_at = layouts
    pairs = residue.shape[0]
    blocks = 2 * pairs
    out_shape = (pairs, 4, PAIR, HEAD_DIM)

    def body(
        k_load_ref, v_load_ref, store_ref, residue_ref, offsets_ref, packed_ref, out_ref, k_sum, v_sum
    ):
        @pl.when(pl.program_id(0) == 0)
        def _():
            k_sum[...] = jnp.zeros(k_sum.shape, f32)
            v_sum[...] = jnp.zeros(v_sum.shape, f32)

        first = pl.program_id(0) * PAIRS_AT_ONCE
        held = {}
        weights = {}
        products = {}

        def scores(u):
            q_rows = pair_queries(packed_ref, q_at, first + u)
            held[u] = pair_scores(k_load_ref, q_rows, packed_ref, first + u)
            grads = pair_queries(packed_ref, g_at, first + u)
            products[u] = pair_dweights(v_load_ref, packed_ref, grads, first + u)

        def softmax(u):
            weights[u] = pair_weights(residue_ref, offsets_ref, held[u], first + u)

        def attend(u):
            out = rows_of_pair(weights[u], packed_ref, v_load_ref, first + u).astype(bf16)
            out_ref[first + u, 0] = out
            grads = pair_queries(packed_ref, g_at, first + u)
            held[u] = pair_dscores(weights[u], products.pop(u), grads, out)

        def dvalues(u):
            grads = pair_queries(packed_ref, g_at, first + u)
            parts = lax.dot_general(
                weights.pop(u), side_by_side(grads), NN, preferred_element_type=f32
            )
            add_to_listed(v_sum, parts, store_ref, 2 * (first + u))

        def dqk(u):
            q_diag = side_by_side(pair_queries(packed_ref, q_at, first + u))
            parts = lax.dot_general(held[u], q_diag, NN, preferred_element_type=f32)
            add_to_listed(k_sum, parts, store_ref, 2 * (first + u))
            out = rows_of_pair(held.pop(u), packed_ref, k_load_ref, first + u)
            out_ref[first + u, 1] = (out * SCALE).astype(bf16)

        staggered(PAIRS_AT_ONCE, (scores, softmax, attend, dvalues, dqk))

        @pl.when(pl.program_id(0) == pl.num_programs(0) - 1)
        def _():
            by_pair = (pairs, PAIR, HEAD_DIM)
            out_ref[:, 2] = (k_sum[:blocks] * SCALE).astype(bf16).reshape(by_pair)
            out_ref[:, 3] = v_sum[:blocks].astype(bf16).reshape(by_pair)

    return pl.pallas_call(
        body,
        grid=(pairs // PAIRS_AT_ONCE,),
        in_specs=[SCALARS] * 3 + [resident(residue.shape), resident(offsets.shape), IN_VMEM],
        out_specs=resident(out_shape),
        out_shape=jax.ShapeDtypeStruct(out_shape, bf16),
        scratch_shapes=[pltpu.VMEM((blocks + 1, BLOCK, HEAD_DIM), f32)] * 2,
        cost_estimate=pl.CostEstimate(
            flops=44_000_000_000, transcendentals=3_000_000, bytes_accessed=10_000_000
        ),
        compiler_params=pltpu.CompilerParams(vmem_limit_bytes=VMEM_LIMIT),
        name="head_at_once",
    )(k_load, v_load, store, residue, offsets, packed)


def exchange(by_device):
    return lax.all_to_all(by_device, "seq", split_axis=0, concat_axis=0, tiled=True)


def in_hbm(array):
    return pltpu.with_memory_space_constraint(array, pltpu.HBM)


def pack_heads(*arrays):
    tokens, width = arrays[0].shape
    number = len(arrays)

    def body(*refs):
        for a in range(number):
            for h in range(HEADS_PER_STEP):
                refs[number][h, a] = refs[a][:, h * HEAD_DIM : (h + 1) * HEAD_DIM]

    return pl.pallas_call(
        body,
        grid=(width // HEAD_DIM // HEADS_PER_STEP,),
        in_specs=[pl.BlockSpec((tokens, HEADS_PER_STEP * HEAD_DIM), lambda step: (0, step))]
        * number,
        out_specs=pl.BlockSpec(
            (HEADS_PER_STEP, number, tokens, HEAD_DIM), lambda step: (step, 0, 0, 0)
        ),
        out_shape=pltpu.HBM((width // HEAD_DIM, number, tokens, HEAD_DIM), bf16),
        compiler_params=pltpu.CompilerParams(vmem_limit_bytes=24 << 20),
        name="pack_heads",
    )(*[in_hbm(x) for x in arrays])


def unpack_heads(packed):
    heads, number, tokens, _ = packed.shape

    def body(packed_ref, *out_refs):
        for a in range(number):
            for h in range(HEADS_PER_STEP):
                out_refs[a][:, h * HEAD_DIM : (h + 1) * HEAD_DIM] = packed_ref[h, a]

    return pl.pallas_call(
        body,
        grid=(heads // HEADS_PER_STEP,),
        in_specs=[
            pl.BlockSpec((HEADS_PER_STEP, number, tokens, HEAD_DIM), lambda step: (step, 0, 0, 0))
        ],
        out_specs=[pl.BlockSpec((tokens, HEADS_PER_STEP * HEAD_DIM), lambda step: (0, step))]
        * number,
        out_shape=[jax.ShapeDtypeStruct((tokens, heads * HEAD_DIM), bf16)] * number,
        compiler_params=pltpu.CompilerParams(vmem_limit_bytes=24 << 20),
        name="unpack_heads",
    )(packed)


def after(first, *later):
    return lax.optimization_barrier((first,) + later)[1:]


def one_head(portions, layouts, queries, keys, values, out_grad, key_blocks, dilation):
    arrays = (queries, keys, values)
    packed = []
    for portion in portions:
        sources = [arrays[i] for i in portion]
        if packed:
            sources = after(packed[-1][:1, :1, :1, :1], *sources)
        packed.append(exchange(pack_heads(*sources)))
    packed = [x.reshape(-1, BLOCK, HEAD_DIM) for x in packed]
    my_head = lax.axis_index("seq")
    lists, store, residue, offsets = index_tables(
        lax.dynamic_index_in_dim(key_blocks, my_head, 0, keepdims=False),
        lax.dynamic_index_in_dim(dilation, my_head, 0, keepdims=False),
    )
    tables = (layouts[1].positions(lists), layouts[2].positions(lists), store, residue, offsets)
    tables = tuple(in_hbm(x) for x in tables)
    packed_grad, tables = lax.optimization_barrier((pack_heads(out_grad), tables))
    g = exchange(packed_grad).reshape(-1, PAIR, HEAD_DIM)
    weights, o = head_forward(packed, layouts, tables)
    attended = exchange(o[:, None])
    grads = exchange(head_backward(packed, layouts, g, o, weights, tables))
    return tuple(unpack_heads(in_hbm(attended))) + tuple(unpack_heads(grads))


def two_exchanges(queries, keys, values, out_grad, key_blocks, dilation):
    layouts = tuple(Packed(0, 4, i) for i in range(4))
    my_head = lax.axis_index("seq")
    lists, store, residue, offsets = index_tables(
        lax.dynamic_index_in_dim(key_blocks, my_head, 0, keepdims=False),
        lax.dynamic_index_in_dim(dilation, my_head, 0, keepdims=False),
    )
    tables = (layouts[1].positions(lists), layouts[2].positions(lists), store, residue, offsets)
    packed = exchange(pack_heads(queries, keys, values, out_grad)).reshape(-1, BLOCK, HEAD_DIM)
    return tuple(unpack_heads(exchange(head_at_once(packed, layouts, tables))))


ALL_AT_ONCE = functools.partial(
    one_head, ((0, 1, 2),), (Packed(0, 3, 0), Packed(0, 3, 1), Packed(0, 3, 2))
)
VALUES_FIRST = functools.partial(
    one_head, ((2,), (0, 1)), (Packed(1, 2, 0), Packed(1, 2, 1), Packed(0, 1, 0))
)


def local(*arguments):
    odd = lax.axis_index("batch") % 2
    return lax.cond(odd == 0, ALL_AT_ONCE, two_exchanges, *arguments)


def solution(mesh):
    rows = P(("batch", "seq"), None)
    return jax.shard_map(
        local,
        mesh=mesh,
        in_specs=(rows, rows, rows, rows, P("batch", None, None), P("batch")),
        out_specs=(rows, rows, rows, rows),
        check_vma=False,
    )
```
